32 devices in a mesh: slab: 2 (over y), tp: 4 (over x, core), band: 4 (over z).
Axes of the slice: x: 2, y: 2, z: 4, core: 2. Of those that a mesh axis runs over, the one named last changes fastest.
Arguments:
- tokens: bfloat16 [3072, 3072], P(('slab', 'band'), 'tp'), may hold values from -6 to 6
- w_qkv: bfloat16 [3072, 3, 3072], P('band', None, 'tp'), may hold values from -0.109375 to 0.109375
- w_out: bfloat16 [3072, 3072], P('tp'), may hold values from -0.109375 to 0.109375
- shift: float32 [3072], replicated, may hold values from -3 to 3
- scale: float32 [3072], replicated, may hold values from -0.9 to 0.9
- gate: float32 [3072], P('tp'), may hold values from 0.5 to 2
- q_gain: float32 [128], replicated, may hold values from 0.5 to 5.5
- k_gain: float32 [128], replicated, may hold values from 0.5 to 5.5
- tile_ids: int32 [24, 14], P(('slab', 'band')), may hold values from 0 to 23, as said below
- key_counts: int32 [24], P(('slab', 'band')), may hold values from 1 to 14, as said below
Outputs:
- update: bfloat16 [3072, 3072], P(('slab', 'band'), 'tp')
The draws below stay inside these ranges and needn't reach their ends.
Inputs may be any that keep to these rules, and one draw needn't show every extreme that they name: `tile_ids`: row q's first key_counts[q] entries are distinct tiles, the first being q itself, whose time index (tile // 12), row index ((tile // 3) % 4) and column index (tile % 3) each differ from q's by at most one; the remaining entries equal q. `key_counts`: 14 is reached in every draw.
All inputs are finite; a program needn't handle non-finite values.
Results may differ from the reference program's by a relative error of at most 0.014.
The reference program's roundings to bfloat16 on the way (of `normed`, `queries`, `keys`, `values`, `probs` and `attended`) count: a program that leaves them out, or rounds other values in their place, can miss the bound.
Values may be sent and summed in bfloat16 or wider, within the bound.
A program may use at most 128 MiB of HBM per device.

```python
import jax
import jax.numpy as jnp
from jax import lax

D = 3072
HD = 128
HEADS = 24
TC = 3
TILE = 128
WIN = 14
TT = 2
TR = 4
NTILES = 24
TOKENS = 3072


def pattern_tables(key):
    local_key = jax.random.fold_in(key, 71)
    first_key, second_key = jax.random.split(local_key)
    tile = jnp.arange(NTILES, dtype=jnp.int32)
    time_pos = tile // (TR * TC)
    row_pos = tile // TC % TR
    column_pos = tile % TC
    offset = jnp.arange(27, dtype=jnp.int32)
    time_near = time_pos[:, None] + offset[None, :] // 9 - 1
    row_near = row_pos[:, None] + offset[None, :] // 3 % 3 - 1
    column_near = column_pos[:, None] + offset[None, :] % 3 - 1
    inside = (time_near >= 0) & (time_near < TT) & (row_near >= 0) & (row_near < TR)
    inside = inside & (column_near >= 0) & (column_near < TC)
    near_id = (time_near * TR + row_near) * TC + column_near
    noise = jax.random.randint(first_key, (NTILES, 27), 0, 2 ** 20)
    priority = jnp.where(offset[None, :] == 13, 2 ** 30, 0) + inside.astype(jnp.int32) * 2 ** 26 + noise * 32 + offset[None, :]
    unused, order = lax.top_k(priority, WIN)
    chosen = jnp.take_along_axis(near_id, order, axis=1)
    upper = jnp.minimum(jnp.sum(inside.astype(jnp.int32), axis=1), WIN)
    number = jax.random.randint(second_key, (NTILES,), 1, upper + 1)
    number = jnp.where(tile == TC + 1, WIN, number).astype(jnp.int32)
    slot_ids = jnp.arange(WIN, dtype=jnp.int32)
    listed = jnp.where(slot_ids[None, :] < number[:, None], chosen, tile[:, None])
    return (listed.astype(jnp.int32), number)


def draw_tile_ids(key, part):
    return pattern_tables(key)[0]


def draw_key_counts(key, part):
    return pattern_tables(key)[1]


def gain_draw(key):
    return jax.random.uniform(key, (HD,), jnp.float32, 0.6, 1.6)


def draw_q_gain(key, part):
    return gain_draw(jax.random.fold_in(key, 11))


def draw_k_gain(key, part):
    return gain_draw(jax.random.fold_in(key, 13))


def block_scale(rng, dims, cuts, least, high):
    loudness = 1.0
    for axis_at, blocks in cuts:
        draws = jax.random.uniform(jax.random.fold_in(jax.random.fold_in(rng, 6), axis_at), (blocks,), jnp.float32, least / len(cuts), high / len(cuts))
        loudness = loudness * jnp.repeat(jnp.exp(draws), dims[axis_at] // blocks).reshape((-1,) + (1,) * (len(dims) - 1 - axis_at))
    return loudness


def normal_values(key, shape, scale, most, pieces=(), kind=jnp.bfloat16):
    entries = scale * jax.random.normal(key, shape, jnp.float32)
    if pieces:
        entries = entries * block_scale(key, shape, pieces, -0.22, 0.18)
    return jnp.clip(entries, -most, most).astype(kind)


def setup_inputs(seed: int = 0) -> dict:
    key_list = jax.random.split(jax.random.key(seed), 11)
    return {
        "tokens": normal_values(key_list[0], (TOKENS, D), 1.0, 6.0, ((0, 8), (1, 4))),
        "w_qkv": normal_values(key_list[1], (D, 3, D), D ** -0.5, 0.109375, ((0, 4), (2, 4))),
        "w_out": normal_values(key_list[2], (D, D), D ** -0.5, 0.109375, ((0, 4),)),
        "shift": normal_values(key_list[3], (D,), 0.5, 3.0, (), jnp.float32),
        "scale": normal_values(key_list[4], (D,), 0.3, 0.9, (), jnp.float32),
        "gate": jnp.clip(0.5 + 1.5 * jax.random.uniform(key_list[5], (D,), jnp.float32) ** block_scale(key_list[5], (D,), ((0, 4),), -0.2, 0.2), 0.5, 2.0),
        "q_gain": draw_q_gain(jax.random.fold_in(key_list[10], 71), 0),
        "k_gain": draw_k_gain(jax.random.fold_in(key_list[10], 71), 0),
        "tile_ids": draw_tile_ids(jax.random.fold_in(key_list[10], 71), 0),
        "key_counts": draw_key_counts(jax.random.fold_in(key_list[10], 71), 0),
    }


def head_norm(part, gain):
    squares = lax.optimization_barrier(jnp.mean(part * part, axis=-1, keepdims=True))
    return (part * lax.rsqrt(squares + 1e-06) * gain).astype(jnp.bfloat16)

def reference(tokens, w_qkv, w_out, shift, scale, gate, q_gain, k_gain, tile_ids, key_counts):
    floats = tokens.astype(jnp.float32)
    center = lax.optimization_barrier(jnp.mean(floats, axis=-1, keepdims=True))
    spread = lax.optimization_barrier(jnp.mean((floats - center) ** 2, axis=-1, keepdims=True))
    normed = ((floats - center) * lax.rsqrt(spread + 1e-06) * (1.0 + scale) + shift).astype(jnp.bfloat16)
    projected = jnp.dot(normed, w_qkv.reshape(D, 3 * D), preferred_element_type=jnp.float32)
    projected = projected.reshape(TOKENS, 3, HEADS, HD)
    queries = head_norm(projected[:, 0], q_gain)
    keys = head_norm(projected[:, 1], k_gain)
    values = projected[:, 2].astype(jnp.bfloat16)
    query_tiles = queries.reshape(NTILES, TILE, HEADS, HD)
    key_tiles = keys.reshape(NTILES, TILE, HEADS, HD)
    value_tiles = values.reshape(NTILES, TILE, HEADS, HD)
    inverse = 1.0 / HD ** 0.5

    def one_tile(items):
        listed, number, query = items
        near_keys = jnp.take(key_tiles, listed, axis=0).astype(jnp.float32)
        near_values = jnp.take(value_tiles, listed, axis=0).astype(jnp.float32)
        scores = jnp.einsum('qhd,wkhd->hqwk', query.astype(jnp.float32), near_keys) * inverse
        allowed = (jnp.arange(WIN) < number)[None, None, :, None]
        scores = jnp.where(allowed, scores, -1e+30)
        top = lax.optimization_barrier(jnp.max(scores, axis=(2, 3), keepdims=True))
        weights = jnp.exp(scores - top)
        probs = (weights / lax.optimization_barrier(jnp.sum(weights, axis=(2, 3), keepdims=True))).astype(jnp.bfloat16)
        result = jnp.einsum('hqwk,wkhd->qhd', probs.astype(jnp.float32), near_values)
        return result.astype(jnp.bfloat16)
    attended = lax.map(one_tile, (tile_ids, key_counts, query_tiles)).reshape(TOKENS, D)
    product = jnp.dot(attended, w_out, preferred_element_type=jnp.float32)
    return (gate * product).astype(jnp.bfloat16)
```

```python
import functools

import jax
import jax.numpy as jnp
from jax import lax
from jax.experimental import pallas as pl
from jax.experimental.pallas import tpu as pltpu
from jax.sharding import PartitionSpec as P

BF = jnp.bfloat16
F32 = jnp.float32


def head_norm(piece, gain):
    squares = jnp.mean(piece * piece, axis=-1, keepdims=True)
    return (piece * lax.rsqrt(squares + 1e-06) * gain).astype(BF)


def attend_kernel(dims, tok_in, w_qkv, scale, shift, q_gain, k_gain, lists_in, att, w_in, tok, w_all,
                  relay, normed, queries, kvs, scores, lists_v, lists_s, place_s, z_send, z_recv, p_send,
                  p_recv, up_send, fwd_send, core_send, w_recv, kv_send, kv_recv, l_send, l_recv,
                  local, w_sem):
    slabs, tps, heads, tiles, slots = dims
    s, t, b = lax.axis_index("slab"), lax.axis_index("tp"), lax.axis_index("band")
    e, c = s % 2, t % 2
    base = s - e
    couples, couple = tps // 2, t // 2
    kind = pl.DeviceIdType.MESH
    head_size = q_gain.shape[1]
    tok_rows, tok_width = tok_in.shape
    tile_len = tok_rows // tiles
    groups = 4 if slabs > 2 else 2
    band_here = 2 * (b % 2) + c
    alone = (c == b // 2) & (c == b % 2)
    other = s + 1 - 2 * e

    def dev(slab, tp, band):
        return {"slab": slab, "tp": tp, "band": band}

    def remote(src, dst, send, recv, peer):
        return pltpu.make_async_remote_copy(src, dst, send, recv, device_id=peer, device_id_type=kind)

    to_t, to_b = 2 * couple + b // 2, 2 * (b % 2) + c
    from_t, from_b = 2 * couple + b % 2, 2 * c + b // 2
    partner = dev(s, t + 1 - 2 * c, b)

    steps = [(0, 1), (0, -1)]
    if slabs > 2:
        steps += [(p, g) for p in (1, -1) for g in (0, 1, -1)]

    def neighbour(p, g):
        at = band_here + g
        there = (at >= 0) & (at <= 3)
        if p:
            there = there & (s + 2 * p >= 0) & (s + 2 * p < slabs)
        at = jnp.clip(at, 0, 3)
        slab = jnp.clip(s + 2 * p, 0, slabs - 1) if p else s
        return dev(slab, 2 * couple + at % 2, 2 * (b // 2) + at // 2), there

    def load(h, i):
        first = pl.multiple_of(e * heads * head_size + h * head_size, head_size)
        cols = slice(i * head_size, (i + 1) * head_size)
        return pltpu.make_async_copy(
            w_qkv.at[i, :, pl.ds(first, head_size)], w_in.at[h, :, cols], w_sem.at[h, i]
        )

    for h in range(heads):
        for i in range(3):
            load(h, i).start()

    barrier = pltpu.get_barrier_semaphore()

    def greet(peer):
        pl.semaphore_signal(barrier, inc=1, device_id=peer, device_id_type=kind)

    peers = [dev(s, t, (b + i) % 4) for i in range(1, 4)]
    for i in range(2):
        for j in range(tps):
            if i or j:
                peers.append(dev(base + (e + i) % 2, (t + j) % tps, b))
    peers += [dev(other, to_t, to_b), dev(other, from_t, from_b)]
    for peer in peers:
        greet(peer)
    expected = len(peers) + jnp.where(alone, 0, 2)

    @pl.when(jnp.logical_not(alone))
    def _():
        greet(dev(s, to_t, to_b))
        greet(dev(s, from_t, from_b))

    for p, g in steps:
        peer, there = neighbour(p, g)
        expected = expected + jnp.where(there, 1, 0)

        @pl.when(there)
        def _(peer=peer):
            greet(peer)

    pl.semaphore_wait(barrier, expected)

    planes = [b // 2, 2 + b // 2]
    legs = [
        remote(tok_in, relay.at[b % 2], z_send.at[i], z_recv.at[b % 2], dev(s, t, planes[i]))
        for i in range(2)
    ]
    for i in range(2):

        @pl.when(planes[i] != b)
        def _(leg=legs[i]):
            leg.start()

    list_home = remote(lists_in, lists_v.at[e], l_send.at[0], l_recv.at[e], dev(s, from_t, from_b))
    list_away = remote(lists_in, lists_v.at[e], l_send.at[1], l_recv.at[e], dev(other, from_t, from_b))
    list_here = pltpu.make_async_copy(lists_in, lists_v.at[e], local.at[0])
    list_away.start()

    @pl.when(alone)
    def _():
        list_here.start()

    @pl.when(jnp.logical_not(alone))
    def _():
        list_home.start()

    u = jnp.where(c == 1, b, 3 - b)

    def at_u(where):
        return dev(s, t, jnp.where(c == 1, where, 3 - where))

    def slot(at):
        return jnp.where(c == 1, at, 3 - at)

    def own(h, where):
        target = 3 if where == 2 else 2
        return remote(w_in.at[h], w_all.at[h, b], up_send.at[h], w_recv.at[b, h], at_u(target))

    def forward(h, at):
        place = slot(at)
        return remote(w_all.at[h, place], w_all.at[h, place], fwd_send.at[at, h], w_recv.at[place, h], at_u(3))

    def across(src, h, at):
        place = slot(at)
        return remote(src, w_all.at[h, place], core_send.at[at, h], w_recv.at[place, h], partner)

    def arrived(h, place):
        return remote(w_in.at[h], w_all.at[h, place], up_send.at[h], w_recv.at[place, h], partner)

    keep = pltpu.make_async_copy(w_in, w_all.at[:, b], local.at[1])
    for where in range(4):

        @pl.when(u == where)
        def _(where=where):
            for h in range(heads):
                for i in range(3):
                    load(h, i).wait()
                own(h, where).start()
                if where >= 2:
                    across(w_in.at[h], h, where).start()
            if where >= 2:
                keep.start()

    def spread(src, q):
        copies = []
        for i in range(2):
            for j in range(couples):
                peer = dev(base + (e + i) % 2, 2 * ((couple + j) % couples) + q, b)
                copies.append(remote(
                    src, tok.at[e, t], p_send.at[q, i * couples + j], p_recv.at[e, t], peer
                ))
        return copies, pltpu.make_async_copy(src, tok.at[e, t], local.at[2])

    for n in range(2):
        q = jnp.where(b < 2, n, 1 - n)
        source = 2 * (b % 2) + q

        def send(src, q=q):
            copies, here = spread(src, q)
            for copy in copies[1:]:
                copy.start()

            @pl.when(c == q)
            def _():
                here.start()

            @pl.when(c != q)
            def _():
                copies[0].start()

        @pl.when(source == b)
        def _(send=send):
            send(tok_in)

        @pl.when(source != b)
        def _(send=send, q=q):
            remote(tok_in, relay.at[q], z_send.at[0], z_recv.at[q], partner).wait_recv()
            send(relay.at[q])

    def serve(h):
        @pl.when(u == 2)
        def _():
            for at in (1, 0):
                arrived(h, slot(at)).wait_recv()
                forward(h, at).start()
                across(w_all.at[h, slot(at)], h, at).start()
            arrived(h, slot(3)).wait_recv()
            across(w_all.at[h, slot(3)], h, 3).start()

        @pl.when(u == 3)
        def _():
            for at in (2, 1, 0):
                arrived(h, slot(at)).wait_recv()
                across(w_all.at[h, slot(at)], h, at).start()

        @pl.when(u < 2)
        def _():
            for at in range(4):
                arrived(h, at).wait_recv()

    serve(0)

    remote(lists_in, lists_v.at[1 - e], l_send.at[0], l_recv.at[1 - e], partner).wait_recv()

    @pl.when(alone)
    def _():
        list_here.wait()

    @pl.when(jnp.logical_not(alone))
    def _():
        remote(lists_in, lists_v.at[e], l_send.at[0], l_recv.at[e], partner).wait_recv()

    down = pltpu.make_async_copy(lists_v, lists_s, local.at[3])
    down.start()
    down.wait()

    def set_places(tile, carry):
        half, i = tile // tiles, tile % tiles
        for j in range(slots):
            listed = lists_s[half, i, j]
            near = listed // (4 * tiles) - base
            group = jnp.where(near < 0, 2, jnp.where(near > 1, 3, near))
            row = listed // tiles % 4 - band_here + 1
            place = (row * groups + group) * tiles + listed % tiles
            place_s[tile, j] = jnp.clip(place, 0, 3 * groups * tiles - 1)
        place_s[tile, slots] = lists_s[half, i, slots]
        return carry

    lax.fori_loop(0, 2 * tiles, set_places, 0)

    for i in range(2):
        for j in range(tps):
            if i or j:
                from_e, from_t2 = (e + i) % 2, (t + j) % tps
                remote(
                    tok_in, tok.at[from_e, from_t2], p_send.at[0, 0], p_recv.at[from_e, from_t2], partner
                ).wait_recv()
    spread(tok_in, c)[1].wait()
    block = 64
    many = tok_rows // block

    def norm_rows(n, carry):
        half, i = n // many, n % many
        rows = pl.ds(pl.multiple_of(i * block, block), block)
        floats = jnp.concatenate([tok[half, j, rows, :] for j in range(tps)], axis=1).astype(F32)
        moved = floats - jnp.mean(floats, axis=-1, keepdims=True)
        spread_of = jnp.mean(moved * moved, axis=-1, keepdims=True)
        normed[pl.ds(pl.multiple_of(n * block, block), block), :] = (
            moved * lax.rsqrt(spread_of + 1e-06) * (1.0 + scale[...]) + shift[...]
        ).astype(BF)
        return carry

    lax.fori_loop(0, 2 * many, norm_rows, 0)

    @pl.when(u >= 2)
    def _():
        keep.wait()

    home = groups * tiles

    def project(h):
        def rows_of(half, carry):
            rows = pl.ds(pl.multiple_of(half * tok_rows, tok_rows), tok_rows)
            weights = w_all[h].reshape(normed.shape[1], w_all.shape[3])
            product = jnp.dot(normed[rows, :], weights, preferred_element_type=F32)
            queries[h, rows, :] = head_norm(product[:, :head_size], q_gain[...])
            keys = head_norm(product[:, head_size : 2 * head_size], k_gain[...])
            values = product[:, 2 * head_size :].astype(BF)
            for i in range(tiles):
                part = slice(i * tile_len, (i + 1) * tile_len)
                kvs[h][home + half * tiles + i, :, :head_size] = keys[part]
                kvs[h][home + half * tiles + i, :, head_size:] = values[part]
            return carry

        lax.fori_loop(0, 2, rows_of, 0)

    def share(h, n):
        p, g = steps[n]
        peer, there = neighbour(p, g)
        if p == 0:
            first, count, group = home, 2 * tiles, 0
        else:
            first, count, group = home + (tiles if p == 1 else 0), tiles, (2 if p == 1 else 3)
        target = (1 - g) * home + group * tiles
        copy = remote(
            kvs[h].at[pl.ds(first, count)], kvs[h].at[pl.ds(target, count)],
            kv_send.at[h, n], kv_recv.at[h, n], peer,
        )
        return copy, there

    def share_all(h):
        for n in range(len(steps)):
            copy, there = share(h, n)

            @pl.when(there)
            def _(copy=copy):
                copy.start()

    def shared(h):
        for n, (p, g) in enumerate(steps):
            copy, _ = share(h, n)
            _, there = neighbour(-p, -g)

            @pl.when(there)
            def _(copy=copy):
                copy.wait_recv()

    inverse = 1.0 / head_size**0.5
    pair = 2 * tile_len
    lane = lax.broadcasted_iota(jnp.int32, (1, pair), 1)

    def attend(h):
        kv = kvs[h]

        def near(tile, j, first):
            parts = []
            for i in range(2):
                at = place_s[tile, min(2 * j + i, slots - 1)]
                parts.append(kv[at, :, first : first + head_size])
            return jnp.concatenate(parts, axis=0)

        def tile_of(i, half):
            tile = half * tiles + i
            rows = pl.ds(pl.multiple_of(tile * tile_len, tile_len), tile_len)
            query = queries[h, rows, :]
            limit = place_s[tile, slots] * tile_len
            trips = (slots + 1) // 2
            top = None
            for j in range(trips):
                found = lax.dot_general(
                    query, near(tile, j, 0), (((1,), (1,)), ((), ())), preferred_element_type=F32
                )
                found = jnp.where(lane < limit - pair * j, found * inverse, -1e30)
                scores[half, :, j * pair : (j + 1) * pair] = found
                top = found if top is None else jnp.maximum(top, found)
            top = jnp.max(top, axis=-1, keepdims=True)
            total = None
            for j in range(trips):
                weights = jnp.exp(scores[half, :, j * pair : (j + 1) * pair] - top)
                scores[half, :, j * pair : (j + 1) * pair] = weights
                total = weights if total is None else total + weights
            part = 1.0 / jnp.sum(total, axis=-1, keepdims=True)
            result = None
            for j in range(trips):
                probs = (scores[half, :, j * pair : (j + 1) * pair] * part).astype(BF)
                found = jnp.dot(probs, near(tile, j, head_size), preferred_element_type=F32)
                result = found if result is None else result + found
            at = pl.ds(pl.multiple_of(i * tile_len, tile_len), tile_len)
            att[half, at, h * head_size : (h + 1) * head_size] = result.astype(BF)

        def both(i, carry):
            tile_of(i, 0)
            tile_of(i, 1)
            return carry

        lax.fori_loop(0, tiles, both, 0)

    for h in range(heads):
        if h:
            serve(h)
        project(h)
        share_all(h)
        if h:
            shared(h - 1)
            attend(h - 1)
    shared(heads - 1)
    attend(heads - 1)

    for where in range(4):

        @pl.when(u == where)
        def _(where=where):
            for h in range(heads):
                own(h, where).wait_send()
                if where == 2:
                    for at in (1, 0):
                        forward(h, at).wait_send()
                if where >= 2:
                    for at in range(4):
                        across(w_in.at[h], h, at).wait_send()

    for i in range(2):

        @pl.when(planes[i] != b)
        def _(leg=legs[i]):
            leg.wait_send()

    for q in range(2):
        copies, _ = spread(tok_in, q)
        for copy in copies[1:]:
            copy.wait_send()

        @pl.when(c != q)
        def _(copy=copies[0]):
            copy.wait_send()

    list_away.wait_send()

    @pl.when(jnp.logical_not(alone))
    def _():
        list_home.wait_send()

    for h in range(heads):
        for n in range(len(steps)):
            copy, there = share(h, n)

            @pl.when(there)
            def _(copy=copy):
                copy.wait_send()


def attended(tokens, w, scale, shift, q_gain, k_gain, lists, slabs, tps, tiles, slots):
    tok_rows, tok_width = tokens.shape
    head_size = q_gain.shape[0]
    heads, deep, wide = w.shape[2] // head_size // 2, w.shape[1], 3 * head_size
    tile_len = tok_rows // tiles
    width = scale.shape[0]
    groups = 4 if slabs > 2 else 2
    steps = 8 if slabs > 2 else 2
    dma = pltpu.SemaphoreType.DMA
    vmem = pl.BlockSpec(memory_space=pltpu.VMEM)
    return pl.pallas_call(
        functools.partial(attend_kernel, (slabs, tps, heads, tiles, slots)),
        out_shape=jax.ShapeDtypeStruct((2, tok_rows, heads * head_size), BF),
        in_specs=[vmem, pl.BlockSpec(memory_space=pl.ANY)] + [vmem] * 5,
        out_specs=vmem,
        scratch_shapes=[
            pltpu.VMEM((heads, deep, wide), BF),
            pltpu.VMEM((2, tps) + tokens.shape, BF),
            pltpu.VMEM((heads, 4, deep, wide), BF),
            pltpu.VMEM((2,) + tokens.shape, BF),
            pltpu.VMEM((2 * tok_rows, width), BF),
            pltpu.VMEM((heads, 2 * tok_rows, head_size), BF),
            [pltpu.VMEM((3 * groups * tiles, tile_len, 2 * head_size), BF) for _ in range(heads)],
            pltpu.VMEM((2, tile_len, (slots + 1) // 2 * 2 * tile_len), F32),
            pltpu.VMEM((2,) + lists.shape, jnp.int32),
            pltpu.SMEM((2,) + lists.shape, jnp.int32),
            pltpu.SMEM((2 * tiles, slots + 1), jnp.int32),
            dma((2,)), dma((2,)), dma((2, tps)), dma((2, tps)),
            dma((heads,)), dma((2, heads)), dma((4, heads)), dma((4, heads)),
            dma((heads, steps)), dma((heads, steps)), dma((2,)), dma((2,)), dma((4,)),
            dma((heads, 3)),
        ],
        compiler_params=pltpu.CompilerParams(
            collective_id=0, has_side_effects=True, vmem_limit_bytes=56 * 2**20
        ),
        name="attended",
    )(
        tokens, w, scale.reshape(1, -1), shift.reshape(1, -1), q_gain.reshape(1, -1),
        k_gain.reshape(1, -1), lists,
    )


def finish_kernel(tps, att, w_out, gate, out, joint, core_out, core_in, far_out, far_in, j_send,
                  j_recv, c_send, c_recv, f_send, f_recv, local):
    s, t, b = lax.axis_index("slab"), lax.axis_index("tp"), lax.axis_index("band")
    e, c = s % 2, t % 2
    couples, couple = tps // 2, t // 2
    half = att.shape[2]
    width = out.shape[1]
    other = s + 1 - 2 * e
    alone = (c == b // 2) & (c == b % 2)
    kind = pl.DeviceIdType.MESH

    def dev(slab, tp, band):
        return {"slab": slab, "tp": tp, "band": band}

    to_t, to_b = 2 * couple + b // 2, 2 * (b % 2) + c
    from_t, from_b = 2 * couple + b % 2, 2 * c + b // 2
    partner = dev(s, t + 1 - 2 * c, b)
    across = [dev(s, 2 * ((couple + j) % couples) + c, b) for j in range(1, couples)]
    barrier = pltpu.get_barrier_semaphore()
    peers = [dev(other, to_t, to_b), dev(other, from_t, from_b), partner] + across
    for peer in peers:
        pl.semaphore_signal(barrier, inc=1, device_id=peer, device_id_type=kind)

    @pl.when(jnp.logical_not(alone))
    def _():
        for peer in (dev(s, to_t, to_b), dev(s, from_t, from_b)):
            pl.semaphore_signal(barrier, inc=1, device_id=peer, device_id_type=kind)

    pl.semaphore_wait(barrier, len(peers) + jnp.where(alone, 0, 2))

    def remote(src, dst, send, recv, peer):
        return pltpu.make_async_remote_copy(src, dst, send, recv, device_id=peer, device_id_type=kind)

    away = remote(att.at[1 - e], joint.at[e], j_send.at[1], j_recv.at[e], dev(other, to_t, to_b))
    home = remote(att.at[e], joint.at[e], j_send.at[0], j_recv.at[e], dev(s, to_t, to_b))
    here = pltpu.make_async_copy(att.at[e], joint.at[e], local.at[0])
    away.start()

    @pl.when(alone)
    def _():
        here.start()
        here.wait()

    @pl.when(jnp.logical_not(alone))
    def _():
        home.start()
        home.wait_send()
        home.wait_recv()

    away.wait_send()
    remote(att.at[e], joint.at[1 - e], j_send.at[1], j_recv.at[1 - e], partner).wait_recv()

    def share(j, core):
        target = 2 * ((couple + j) % couples) + core
        cols = pl.ds(pl.multiple_of(target * width, width), width)
        total = jnp.dot(joint[0], w_out[:half, cols], preferred_element_type=F32)
        return total + jnp.dot(joint[1], w_out[half:, cols], preferred_element_type=F32)

    order = list(range(1, couples)) + [0]
    swaps = [
        remote(core_out.at[j], core_in.at[j], c_send.at[j], c_recv.at[j], partner)
        for j in range(couples)
    ]
    sends = [
        remote(far_out.at[j - 1], far_in.at[j - 1], f_send.at[j - 1], f_recv.at[j - 1], across[j - 1])
        for j in range(1, couples)
    ]
    for j in order[:-1]:
        core_out[j] = share(j, 1 - c)
        swaps[j].start()
        mine = share(j, c)
        swaps[j].wait_recv()
        far_out[j - 1] = (mine + core_in[j]).astype(BF)
        sends[j - 1].start()
    core_out[0] = share(0, 1 - c)
    swaps[0].start()
    total = share(0, c)
    swaps[0].wait_recv()
    core_in[0] = total + core_in[0]
    for j in range(1, couples):
        sends[j - 1].wait_recv()
        core_in[0] += far_in[j - 1].astype(F32)
    out[...] = (gate[...] * core_in[0]).astype(BF)
    for j in range(1, couples):
        sends[j - 1].wait_send()
    for j in range(couples):
        swaps[j].wait_send()


def finish(att, w_out, gate, tps):
    rows, half = att.shape[1:]
    width = gate.shape[0]
    couples = tps // 2
    dma = pltpu.SemaphoreType.DMA
    vmem = pl.BlockSpec(memory_space=pltpu.VMEM)
    return pl.pallas_call(
        functools.partial(finish_kernel, tps),
        out_shape=jax.ShapeDtypeStruct((rows, width), BF),
        in_specs=[vmem] * 3,
        out_specs=vmem,
        scratch_shapes=[
            pltpu.VMEM((2, rows, half), BF),
            pltpu.VMEM((couples, rows, width), F32),
            pltpu.VMEM((couples, rows, width), F32),
            pltpu.VMEM((couples - 1, rows, width), BF),
            pltpu.VMEM((couples - 1, rows, width), BF),
            dma((2,)), dma((2,)), dma((couples,)), dma((couples,)),
            dma((couples - 1,)), dma((couples - 1,)), dma((1,)),
        ],
        compiler_params=pltpu.CompilerParams(collective_id=1, has_side_effects=True),
        name="finish",
    )(att, w_out, gate.reshape(1, -1))


def shards(tokens, w_qkv, w_out, shift, scale, gate, q_gain, k_gain, tile_ids, key_counts):
    slabs, tps = lax.axis_size("slab"), lax.axis_size("tp")
    tiles, slots = tile_ids.shape
    lists = jnp.concatenate([tile_ids, key_counts[:, None]], axis=1)
    lists = jnp.pad(lists, ((0, 8 - tiles), (0, 128 - slots - 1)))
    att = attended(tokens, w_qkv.transpose(1, 0, 2), scale, shift, q_gain, k_gain, lists, slabs, tps, tiles, slots)
    return finish(att, w_out, gate, tps)


def solution(mesh):
    in_specs = (
        P(("slab", "band"), "tp"),
        P("band", None, "tp"),
        P("tp", None),
        P(),
        P(),
        P("tp"),
        P(),
        P(),
        P(("slab", "band"), None),
        P(("slab", "band")),
    )
    out_specs = P(("slab", "band"), "tp")
    return jax.shard_map(shards, mesh=mesh, in_specs=in_specs, out_specs=out_specs, check_vma=False)
```

```python
import functools

import jax
import jax.numpy as jnp
from jax import lax
from jax.experimental import pallas as pl
from jax.experimental.pallas import tpu as pltpu
from jax.sharding import PartitionSpec as P

BF = jnp.bfloat16
F32 = jnp.float32


def head_norm(piece, gain):
    squares = jnp.mean(piece * piece, axis=-1, keepdims=True)
    return (piece * lax.rsqrt(squares + 1e-06) * gain).astype(BF)


def branch_kernel(dims, tok_in, w_qkv, scale, shift, q_gain, k_gain, lists_in, w_out, gate, out, w_in, tok, w_all,
                  relay, normed, queries, kvs, att, joint, w_cols, total, scores, lists_v, lists_s, place_s, z_send, z_recv, p_send,
                  p_recv, turn_send, up_send, fwd_send, core_send, w_recv, kv_send, kv_recv, l_send, l_recv,
                  local, local_t, w_sem,
                  j_send, j_recv, a_send, a_recv, r_send, o_send, o_recv, o_local):
    slabs, tps, heads, tiles, slots = dims
    s, t, b = lax.axis_index("slab"), lax.axis_index("tp"), lax.axis_index("band")
    e, c = s % 2, t % 2
    base = s - e
    couples, couple = tps // 2, t // 2
    kind = pl.DeviceIdType.MESH
    head_size = q_gain.shape[1]
    tok_rows, tok_width = tok_in.shape
    tile_len = tok_rows // tiles
    groups = 4 if slabs > 2 else 2
    band_here = 2 * (b % 2) + c
    alone = (c == b // 2) & (c == b % 2)
    other = s + 1 - 2 * e

    def dev(slab, tp, band):
        return {"slab": slab, "tp": tp, "band": band}

    def remote(src, dst, send, recv, peer):
        return pltpu.make_async_remote_copy(src, dst, send, recv, device_id=peer, device_id_type=kind)

    to_t, to_b = 2 * couple + b // 2, 2 * (b % 2) + c
    from_t, from_b = 2 * couple + b % 2, 2 * c + b // 2
    partner = dev(s, t + 1 - 2 * c, b)

    steps = [(0, 1), (0, -1)]
    if slabs > 2:
        steps += [(p, g) for p in (1, -1) for g in (0, 1, -1)]

    def neighbour(p, g):
        at = band_here + g
        there = (at >= 0) & (at <= 3)
        if p:
            there = there & (s + 2 * p >= 0) & (s + 2 * p < slabs)
        at = jnp.clip(at, 0, 3)
        slab = jnp.clip(s + 2 * p, 0, slabs - 1) if p else s
        return dev(slab, 2 * couple + at % 2, 2 * (b // 2) + at // 2), there

    def load(h, i):
        first = pl.multiple_of(e * heads * head_size + h * head_size, head_size)
        cols = slice(i * head_size, (i + 1) * head_size)
        return pltpu.make_async_copy(
            w_qkv.at[i, :, pl.ds(first, head_size)], w_in.at[h, :, cols], w_sem.at[h, i]
        )

    for h in range(heads):
        for i in range(3):
            load(h, i).start()

    barrier = pltpu.get_barrier_semaphore()

    def greet(peer):
        pl.semaphore_signal(barrier, inc=1, device_id=peer, device_id_type=kind)

    peers = [dev(s, t, (b + i) % 4) for i in range(1, 4)]
    for i in range(2):
        for j in range(tps):
            if i or j:
                peers.append(dev(base + (e + i) % 2, (t + j) % tps, b))
    peers += [dev(other, to_t, to_b), dev(other, from_t, from_b)]
    for peer in peers:
        greet(peer)
    expected = len(peers) + jnp.where(alone, 0, 2)

    @pl.when(jnp.logical_not(alone))
    def _():
        greet(dev(s, to_t, to_b))
        greet(dev(s, from_t, from_b))

    for p, g in steps:
        peer, there = neighbour(p, g)
        expected = expected + jnp.where(there, 1, 0)

        @pl.when(there)
        def _(peer=peer):
            greet(peer)

    pl.semaphore_wait(barrier, expected)

    pieces, piece_rows = tok.shape[2], tok.shape[3]
    planes = [b // 2, 2 + b // 2]

    def part(k):
        return tok_in.at[pl.ds(k * piece_rows, piece_rows)]

    def leg(i, k):
        return remote(
            part(k), relay.at[b % 2, k], z_send.at[i, k], z_recv.at[b % 2, k], dev(s, t, planes[i])
        )

    far_first = [1, 0]
    for i in far_first:

        @pl.when(planes[i] != b)
        def _(i=i):
            for k in range(pieces):
                leg(i, k).start()

    list_home = remote(lists_in, lists_v.at[e], l_send.at[0], l_recv.at[e], dev(s, from_t, from_b))
    list_away = remote(lists_in, lists_v.at[e], l_send.at[1], l_recv.at[e], dev(other, from_t, from_b))
    list_here = pltpu.make_async_copy(lists_in, lists_v.at[e], local.at[0])
    list_away.start()

    @pl.when(alone)
    def _():
        list_here.start()

    @pl.when(jnp.logical_not(alone))
    def _():
        list_home.start()

    u = jnp.where(c == 1, b, 3 - b)

    def at_u(where):
        return dev(s, t, jnp.where(c == 1, where, 3 - where))

    def slot(at):
        return jnp.where(c == 1, at, 3 - at)

    def own(h, where):
        target = 3 if where == 2 else 2
        return remote(w_in.at[h], w_all.at[h, b], up_send.at[h], w_recv.at[b, h], at_u(target))

    def forward(h, at):
        place = slot(at)
        return remote(w_all.at[h, place], w_all.at[h, place], fwd_send.at[at, h], w_recv.at[place, h], at_u(3))

    def across(src, h, at):
        place = slot(at)
        return remote(src, w_all.at[h, place], core_send.at[at, h], w_recv.at[place, h], partner)

    def arrived(h, place):
        return remote(w_in.at[h], w_all.at[h, place], up_send.at[h], w_recv.at[place, h], partner)

    keep = pltpu.make_async_copy(w_in, w_all.at[:, b], local.at[1])
    def begin(where, first, last):
        for h in range(first, last):
            for i in range(3):
                load(h, i).wait()
            own(h, where).start()
            if where >= 2:
                across(w_in.at[h], h, where).start()
        if where >= 2 and last == heads:
            keep.start()

    early = 1
    for where in range(4):

        @pl.when(u == where)
        def _(where=where):
            begin(where, 0, heads if where >= 2 else early)

    def spread(src, q, k):
        targets = [dev(s, 2 * couple + q, b), dev(other, 2 * couple + q, b)]
        targets += [dev(s, 2 * lax.rem(couple + j, couples) + q, b) for j in range(1, couples)]
        copies = [
            remote(src, tok.at[e, t, k], p_send.at[q, k, n], p_recv.at[e, t, k], peer)
            for n, peer in enumerate(targets)
        ]
        return copies, pltpu.make_async_copy(src, tok.at[e, t, k], local_t.at[k])

    def send(src, q, k):
        copies, here = spread(src, q, k)
        for copy in copies[1:]:
            copy.start()

        @pl.when(c == q)
        def _():
            here.start()

        @pl.when(c != q)
        def _():
            copies[0].start()

    def landed(from_e, from_t2, k):
        return remote(
            part(0), tok.at[from_e, from_t2, k], p_send.at[0, 0, 0], p_recv.at[from_e, from_t2, k], partner
        )

    def turn(n, k):
        if k % 2:
            from_t2 = 2 * lax.rem(couple + 1 + n // 2, couples) + n % 2
            return landed(e, from_t2, k), remote(
                tok.at[e, from_t2, k], tok.at[e, from_t2, k], turn_send.at[k, n],
                p_recv.at[e, from_t2, k], dev(other, t, b),
            )
        from_t2, jump = 2 * couple + n % 2, 1 + n // 2
        return landed(1 - e, from_t2, k), remote(
            tok.at[1 - e, from_t2, k], tok.at[1 - e, from_t2, k], turn_send.at[k, n],
            p_recv.at[1 - e, from_t2, k], dev(s, 2 * lax.rem(couple + jump, couples) + c, b),
        )

    turns = 2 * (couples - 1)
    for k in range(pieces):
        for n in range(2):
            q = jnp.where(b < 2, n, 1 - n)
            source = 2 * (b % 2) + q

            @pl.when(source == b)
            def _(q=q, k=k):
                send(part(k), q, k)

            @pl.when(source != b)
            def _(q=q, k=k):
                remote(part(k), relay.at[q, k], z_send.at[0, k], z_recv.at[q, k], partner).wait_recv()
                send(relay.at[q, k], q, k)

    for where in (0, 1):

        @pl.when(u == where)
        def _(where=where):
            begin(where, early, heads)

    def serve_2(h):
        for at in (1, 0):
            arrived(h, slot(at)).wait_recv()
            forward(h, at).start()
            across(w_all.at[h, slot(at)], h, at).start()
        arrived(h, slot(3)).wait_recv()
        across(w_all.at[h, slot(3)], h, 3).start()

    def serve(h):
        if h == heads - 1:

            @pl.when(u == 2)
            def _():
                serve_2(h)

        @pl.when(u == 3)
        def _():
            for at in (2, 1, 0):
                arrived(h, slot(at)).wait_recv()
                across(w_all.at[h, slot(at)], h, at).start()

        @pl.when(u < 2)
        def _():
            for at in range(4):
                arrived(h, at).wait_recv()

    def pass_on(k):
        for m in range(turns):
            here, on = turn(m, k)
            if k % 2 or m < 2:
                here.wait_recv()
            on.start()

    for h in range(heads - 1):
        for k in range(h * pieces // (heads - 1), (h + 1) * pieces // (heads - 1)):
            pass_on(k)

        @pl.when(u == 2)
        def _(h=h):
            serve_2(h)

    out_width = gate.shape[1]

    def out_rows(j, h, half):
        target = lax.rem(t + j, tps)
        rows = pl.ds((half * heads + h) * head_size, head_size)
        src = w_out.at[rows, pl.ds(pl.multiple_of(target * out_width, out_width), out_width)]
        place = pl.multiple_of((2 * t + half) * head_size, head_size)
        dst = w_cols.at[h, pl.ds(place, head_size)]
        if j == 0:
            return pltpu.make_async_copy(src, dst, o_local.at[h, half])
        return remote(src, dst, o_send.at[j, h, half], o_recv.at[h, t, half], dev(s, target, b))

    for h in range(heads):
        for half in range(2):
            for j in range(tps):
                out_rows(j, h, half).start()

    remote(lists_in, lists_v.at[1 - e], l_send.at[0], l_recv.at[1 - e], partner).wait_recv()

    @pl.when(alone)
    def _():
        list_here.wait()

    @pl.when(jnp.logical_not(alone))
    def _():
        remote(lists_in, lists_v.at[e], l_send.at[0], l_recv.at[e], partner).wait_recv()

    down = pltpu.make_async_copy(lists_v, lists_s, local.at[3])
    down.start()
    down.wait()

    def set_places(tile, carry):
        half, i = tile // tiles, tile % tiles
        for j in range(slots):
            listed = lists_s[half, i, j]
            near = listed // (4 * tiles) - base
            group = jnp.where(near < 0, 2, jnp.where(near > 1, 3, near))
            row = listed // tiles % 4 - band_here + 1
            place = (row * groups + group) * tiles + listed % tiles
            place_s[tile, j] = jnp.clip(place, 0, 3 * groups * tiles - 1)
        place_s[tile, slots] = lists_s[half, i, slots]
        return carry

    lax.fori_loop(0, 2 * tiles, set_places, 0)

    block = 64 if piece_rows % 64 == 0 else piece_rows
    many = piece_rows // block

    def norm_piece(n, carry):
        half, k = lax.rem(e + n // pieces, 2), n % pieces

        @pl.when(half == e)
        def _():
            @pl.when(k % 2 == 0)
            def _():
                for j in range(2, tps):
                    landed(e, lax.rem(2 * couple + j, tps), k).wait_recv()

            landed(e, t + 1 - 2 * c, k).wait_recv()
            spread(part(0), c, k)[1].wait()

        @pl.when(half != e)
        def _():
            @pl.when(k % 2 == 1)
            def _():
                for j in range(2):
                    landed(1 - e, 2 * couple + j, k).wait_recv()

            for j in range(2, tps):
                landed(1 - e, lax.rem(2 * couple + j, tps), k).wait_recv()

        def norm_rows(i, inner):
            rows = pl.ds(pl.multiple_of(i * block, block), block)
            floats = jnp.concatenate([tok[half, j, k, rows, :] for j in range(tps)], axis=1).astype(F32)
            moved = floats - jnp.mean(floats, axis=-1, keepdims=True)
            spread_of = jnp.mean(moved * moved, axis=-1, keepdims=True)
            at = ((half * pieces + k) * many + i) * block
            normed[pl.ds(pl.multiple_of(at, block), block), :] = (
                moved * lax.rsqrt(spread_of + 1e-06) * (1.0 + scale[...]) + shift[...]
            ).astype(BF)
            return inner

        lax.fori_loop(0, many, norm_rows, 0)
        return carry

    lax.fori_loop(0, 2 * pieces, norm_piece, 0)

    @pl.when(u >= 2)
    def _():
        keep.wait()

    home = groups * tiles

    def project(h):
        def rows_of(half, carry):
            rows = pl.ds(pl.multiple_of(half * tok_rows, tok_rows), tok_rows)
            weights = w_all[h].reshape(normed.shape[1], w_all.shape[3])
            product = jnp.dot(normed[rows, :], weights, preferred_element_type=F32)
            queries[h, rows, :] = head_norm(product[:, :head_size], q_gain[...])
            keys = head_norm(product[:, head_size : 2 * head_size], k_gain[...])
            values = product[:, 2 * head_size :].astype(BF)
            for i in range(tiles):
                part = slice(i * tile_len, (i + 1) * tile_len)
                kvs[h][home + half * tiles + i, :, :head_size] = keys[part]
                kvs[h][home + half * tiles + i, :, head_size:] = values[part]
            return carry

        lax.fori_loop(0, 2, rows_of, 0)

    def share(h, n):
        p, g = steps[n]
        peer, there = neighbour(p, g)
        if p == 0:
            first, count, group = home, 2 * tiles, 0
        else:
            first, count, group = home + (tiles if p == 1 else 0), tiles, (2 if p == 1 else 3)
        target = (1 - g) * home + group * tiles
        copy = remote(
            kvs[h].at[pl.ds(first, count)], kvs[h].at[pl.ds(target, count)],
            kv_send.at[h, n], kv_recv.at[h, n], peer,
        )
        return copy, there

    def share_all(h):
        for n in range(len(steps)):
            copy, there = share(h, n)

            @pl.when(there)
            def _(copy=copy):
                copy.start()

    def shared(h):
        for n, (p, g) in enumerate(steps):
            copy, _ = share(h, n)
            _, there = neighbour(-p, -g)

            @pl.when(there)
            def _(copy=copy):
                copy.wait_recv()

    inverse = 1.0 / head_size**0.5
    pair = 2 * tile_len
    lane = lax.broadcasted_iota(jnp.int32, (1, pair), 1)

    def attend(h):
        kv = kvs[h]

        def near(tile, j, first):
            parts = []
            for i in range(2):
                at = place_s[tile, min(2 * j + i, slots - 1)]
                parts.append(kv[at, :, first : first + head_size])
            return jnp.concatenate(parts, axis=0)

        def tile_of(i, half):
            tile = half * tiles + i
            rows = pl.ds(pl.multiple_of(tile * tile_len, tile_len), tile_len)
            query = queries[h, rows, :]
            limit = place_s[tile, slots] * tile_len
            trips = (slots + 1) // 2
            top = None
            for j in range(trips):
                found = lax.dot_general(
                    query, near(tile, j, 0), (((1,), (1,)), ((), ())), preferred_element_type=F32
                )
                found = jnp.where(lane < limit - pair * j, found * inverse, -1e30)
                scores[half, :, j * pair : (j + 1) * pair] = found
                top = found if top is None else jnp.maximum(top, found)
            top = jnp.max(top, axis=-1, keepdims=True)
            total = None
            for j in range(trips):
                weights = jnp.exp(scores[half, :, j * pair : (j + 1) * pair] - top)
                scores[half, :, j * pair : (j + 1) * pair] = weights
                total = weights if total is None else total + weights
            part = 1.0 / jnp.sum(total, axis=-1, keepdims=True)
            result = None
            for j in range(trips):
                probs = (scores[half, :, j * pair : (j + 1) * pair] * part).astype(BF)
                found = jnp.dot(probs, near(tile, j, head_size), preferred_element_type=F32)
                result = found if result is None else result + found
            att[h, half, pl.ds(pl.multiple_of(i * tile_len, tile_len), tile_len), :] = result.astype(BF)

        def both(i, carry):
            tile_of(i, 0)
            tile_of(i, 1)
            return carry

        lax.fori_loop(0, tiles, both, 0)

    def deal(h):
        home_copy = remote(
            att.at[h, e], joint.at[h, 2 * to_t + e], j_send.at[h, 0], j_recv.at[h, e], dev(s, to_t, to_b)
        )
        here = pltpu.make_async_copy(att.at[h, e], joint.at[h, 2 * t + e], j_send.at[h, 0])
        away = remote(
            att.at[h, 1 - e], joint.at[h, 2 * to_t + e], j_send.at[h, 1], j_recv.at[h, e],
            dev(other, to_t, to_b),
        )
        return home_copy, here, away

    def start_deal(h):
        home_copy, here, away = deal(h)
        away.start()

        @pl.when(alone)
        def _():
            here.start()

        @pl.when(jnp.logical_not(alone))
        def _():
            home_copy.start()

    def hand(h, part_of, j):
        place = joint.at[h, 2 * t + part_of]
        peer = partner if j == 0 else dev(s, lax.rem(t + 2 * j, tps), b)
        return remote(place, place, a_send.at[h, part_of, j], a_recv.at[h, 2 * t + part_of], peer)

    def handed(h, from_t2, part_of):
        place = joint.at[h, 2 * from_t2 + part_of]
        return remote(
            place, place, r_send.at[h, part_of, from_t2 // 2], a_recv.at[h, 2 * from_t2 + part_of], partner
        )

    def hand_out(h):
        for m in range(2):
            part_of = e if m == 0 else 1 - e

            def arrive():
                remote(
                    att.at[h, 0], joint.at[h, 2 * t + part_of], j_send.at[h, 0], j_recv.at[h, part_of], partner
                ).wait_recv()

            if m == 0:

                @pl.when(alone)
                def _():
                    deal(h)[1].wait()

                @pl.when(jnp.logical_not(alone))
                def _():
                    arrive()
            else:
                arrive()
            for j in range(couples):
                hand(h, part_of, j).start()

    def multiply(h):
        for m in range(2):
            for j in range(1, couples):
                came = handed(h, lax.rem(t + 2 * j, tps), m)
                came.wait_recv()
                came.start()
        for m in range(2):
            handed(h, t + 1 - 2 * c, m).wait_recv()
            for j in range(1, couples):
                handed(h, lax.rem(t + 1 - 2 * c + 2 * j, tps), m).wait_recv()
        for half in range(2):
            for j in range(tps):
                if j:
                    from_t2 = lax.rem(t + j, tps)
                    remote(
                        w_out.at[pl.ds(0, head_size), pl.ds(0, out_width)],
                        w_cols.at[h, pl.ds(pl.multiple_of((2 * from_t2 + half) * head_size, head_size), head_size)],
                        o_send.at[j, h, half], o_recv.at[h, from_t2, half], partner,
                    ).wait_recv()
                else:
                    out_rows(0, h, half).wait()
        whole = jnp.concatenate([joint[h, i] for i in range(2 * tps)], axis=1)
        product = jnp.dot(whole, w_cols[h], preferred_element_type=F32)
        if h == 0:
            total[...] = product
        elif h < heads - 1:
            total[...] += product
        else:
            out[...] = (gate[...] * (total[...] + product)).astype(BF)

    serve(0)
    project(0)
    share_all(0)
    for h in range(1, heads):
        serve(h)
        if h >= 2:
            shared(h - 2)
            attend(h - 2)
            start_deal(h - 2)
        project(h)
        share_all(h)
    shared(heads - 2)
    attend(heads - 2)
    start_deal(heads - 2)
    hand_out(heads - 3)
    shared(heads - 1)
    attend(heads - 1)
    start_deal(heads - 1)
    hand_out(heads - 2)
    for h in range(heads - 1):
        multiply(h)
    hand_out(heads - 1)
    multiply(heads - 1)

    for where in range(4):

        @pl.when(u == where)
        def _(where=where):
            for h in range(heads):
                own(h, where).wait_send()
                if where == 2:
                    for at in (1, 0):
                        forward(h, at).wait_send()
                if where >= 2:
                    for at in range(4):
                        across(w_in.at[h], h, at).wait_send()

    for i in range(2):

        @pl.when(planes[i] != b)
        def _(i=i):
            for k in range(pieces):
                leg(i, k).wait_send()

    for k in range(pieces):
        for q in range(2):
            copies, _ = spread(part(0), q, k)
            for copy in copies[1:]:
                copy.wait_send()

            @pl.when(c != q)
            def _(copy=copies[0]):
                copy.wait_send()

        for m in range(turns):
            turn(m, k)[1].wait_send()

    for h in range(heads):
        home_copy, _, away = deal(h)
        away.wait_send()

        @pl.when(jnp.logical_not(alone))
        def _(home_copy=home_copy):
            home_copy.wait_send()

        for m in range(2):
            for j in range(couples):
                hand(h, m, j).wait_send()
            for j in range(1, couples):
                handed(h, lax.rem(t + 2 * j, tps), m).wait_send()
            for j in range(1, tps):
                out_rows(j, h, m).wait_send()

    list_away.wait_send()

    @pl.when(jnp.logical_not(alone))
    def _():
        list_home.wait_send()

    for h in range(heads):
        for n in range(len(steps)):
            copy, there = share(h, n)

            @pl.when(there)
            def _(copy=copy):
                copy.wait_send()


def branch(tokens, w, scale, shift, q_gain, k_gain, lists, w_out, gate, slabs, tps, tiles, slots):
    tok_rows, tok_width = tokens.shape
    head_size = q_gain.shape[0]
    heads, deep, wide = w.shape[2] // head_size // 2, w.shape[1], 3 * head_size
    tile_len = tok_rows // tiles
    width = scale.shape[0]
    pieces = 4 if tok_rows % 64 == 0 else 2
    groups = 4 if slabs > 2 else 2
    steps = 8 if slabs > 2 else 2
    dma = pltpu.SemaphoreType.DMA
    vmem = pl.BlockSpec(memory_space=pltpu.VMEM)
    return pl.pallas_call(
        functools.partial(branch_kernel, (slabs, tps, heads, tiles, slots)),
        out_shape=jax.ShapeDtypeStruct((tok_rows, gate.shape[0]), BF),
        in_specs=[vmem, pl.BlockSpec(memory_space=pl.ANY)] + [vmem] * 5 + [pl.BlockSpec(memory_space=pl.ANY), vmem],
        out_specs=vmem,
        scratch_shapes=[
            pltpu.VMEM((heads, deep, wide), BF),
            pltpu.VMEM((2, tps, pieces, tok_rows // pieces, tok_width), BF),
            pltpu.VMEM((heads, 4, deep, wide), BF),
            pltpu.VMEM((2, pieces, tok_rows // pieces, tok_width), BF),
            pltpu.VMEM((2 * tok_rows, width), BF),
            pltpu.VMEM((heads, 2 * tok_rows, head_size), BF),
            [pltpu.VMEM((3 * groups * tiles, tile_len, 2 * head_size), BF) for _ in range(heads)],
            pltpu.VMEM((heads, 2, tok_rows, head_size), BF),
            pltpu.VMEM((heads, 2 * tps, tok_rows, head_size), BF),
            pltpu.VMEM((heads, 2 * tps * head_size, gate.shape[0]), BF),
            pltpu.VMEM((tok_rows, gate.shape[0]), F32),
            pltpu.VMEM((2, tile_len, (slots + 1) // 2 * 2 * tile_len), F32),
            pltpu.VMEM((2,) + lists.shape, jnp.int32),
            pltpu.SMEM((2,) + lists.shape, jnp.int32),
            pltpu.SMEM((2 * tiles, slots + 1), jnp.int32),
            dma((2, pieces)), dma((2, pieces)), dma((2, pieces, tps)), dma((2, tps, pieces)),
            dma((pieces, tps)),
            dma((heads,)), dma((2, heads)), dma((4, heads)), dma((4, heads)),
            dma((heads, steps)), dma((heads, steps)), dma((2,)), dma((2,)), dma((4,)), dma((pieces,)),
            dma((heads, 3)),
            dma((heads, 2)), dma((heads, 2)), dma((heads, 2, tps // 2)), dma((heads, 2 * tps)),
            dma((heads, 2, tps // 2)), dma((tps, heads, 2)), dma((heads, tps, 2)), dma((heads, 2)),
        ],
        compiler_params=pltpu.CompilerParams(
            collective_id=0, has_side_effects=True, vmem_limit_bytes=56 * 2**20
        ),
        name="branch",
    )(
        tokens, w, scale.reshape(1, -1), shift.reshape(1, -1), q_gain.reshape(1, -1),
        k_gain.reshape(1, -1), lists, w_out, gate.reshape(1, -1),
    )


def shards(tokens, w_qkv, w_out, shift, scale, gate, q_gain, k_gain, tile_ids, key_counts):
    slabs, tps = lax.axis_size("slab"), lax.axis_size("tp")
    tiles, slots = tile_ids.shape
    lists = jnp.concatenate([tile_ids, key_counts[:, None]], axis=1)
    lists = jnp.pad(lists, ((0, 8 - tiles), (0, 128 - slots - 1)))
    return branch(
        tokens, w_qkv.transpose(1, 0, 2), scale, shift, q_gain, k_gain, lists, w_out, gate,
        slabs, tps, tiles, slots,
    )


def solution(mesh):
    in_specs = (
        P(("slab", "band"), "tp"),
        P("band", None, "tp"),
        P("tp", None),
        P(),
        P(),
        P("tp"),
        P(),
        P(),
        P(("slab", "band"), None),
        P(("slab", "band")),
    )
    out_specs = P(("slab", "band"), "tp")
    return jax.shard_map(shards, mesh=mesh, in_specs=in_specs, out_specs=out_specs, check_vma=False)
```

```python
import functools

import jax
import jax.numpy as jnp
from jax import lax
from jax.experimental import pallas as pl
from jax.experimental.pallas import tpu as pltpu
from jax.sharding import PartitionSpec as P

BF = jnp.bfloat16
F32 = jnp.float32


def head_norm(piece, gain):
    squares = jnp.mean(piece * piece, axis=-1, keepdims=True)
    return (piece * lax.rsqrt(squares + 1e-06) * gain).astype(BF)


def branch_kernel(dims, tok_in, w_qkv, scale, shift, q_gain, k_gain, ids, counts, w_out, out, lists_in, w_in, tok, w_all,
                  relay, normed, queries, kvs, att, joint, w_cols, total, scores, lists_v, lists_s, place_s, z_send, z_recv, p_send,
                  p_recv, turn_send, up_send, fwd_send, core_send, w_recv, kv_send, kv_recv, l_send, l_recv,
                  local, local_t, w_sem,
                  j_send, j_recv, a_send, a_recv, r_send, o_send, o_recv, o_local):
    slabs, tps, heads, tiles, slots = dims
    s, t, b = lax.axis_index("slab"), lax.axis_index("tp"), lax.axis_index("band")
    e, c = s % 2, t % 2
    base = s - e
    couples, couple = tps // 2, t // 2
    kind = pl.DeviceIdType.MESH
    head_size = q_gain.shape[1]
    tok_rows, tok_width = tok_in.shape
    tile_len = tok_rows // tiles
    groups = 4 if slabs > 2 else 2
    band_here = 2 * (b % 2) + c
    alone = (c == b // 2) & (c == b % 2)
    other = s + 1 - 2 * e

    def dev(slab, tp, band):
        return {"slab": slab, "tp": tp, "band": band}

    def remote(src, dst, send, recv, peer):
        return pltpu.make_async_remote_copy(src, dst, send, recv, device_id=peer, device_id_type=kind)

    to_t, to_b = 2 * couple + b // 2, 2 * (b % 2) + c
    from_t, from_b = 2 * couple + b % 2, 2 * c + b // 2
    partner = dev(s, t + 1 - 2 * c, b)

    steps = [(0, 1), (0, -1)]
    if slabs > 2:
        steps += [(p, g) for p in (1, -1) for g in (0, 1, -1)]

    def neighbour(p, g):
        at = band_here + g
        there = (at >= 0) & (at <= 3)
        if p:
            there = there & (s + 2 * p >= 0) & (s + 2 * p < slabs)
        at = jnp.clip(at, 0, 3)
        slab = jnp.clip(s + 2 * p, 0, slabs - 1) if p else s
        return dev(slab, 2 * couple + at % 2, 2 * (b // 2) + at // 2), there

    def load(h, i):
        first = pl.multiple_of(e * heads * head_size + h * head_size, head_size)
        cols = slice(i * head_size, (i + 1) * head_size)
        return pltpu.make_async_copy(
            w_qkv.at[i, :, pl.ds(first, head_size)], w_in.at[h, :, cols], w_sem.at[h, i]
        )

    for h in range(heads):
        for i in range(3):
            load(h, i).start()

    barrier = pltpu.get_barrier_semaphore()

    def greet(peer):
        pl.semaphore_signal(barrier, inc=1, device_id=peer, device_id_type=kind)

    peers = [dev(s, t, (b + i) % 4) for i in range(1, 4)]
    for i in range(2):
        for j in range(tps):
            if i or j:
                peers.append(dev(base + (e + i) % 2, (t + j) % tps, b))
    peers += [dev(other, to_t, to_b), dev(other, from_t, from_b)]
    for peer in peers:
        greet(peer)
    expected = len(peers) + jnp.where(alone, 0, 2)

    @pl.when(jnp.logical_not(alone))
    def _():
        greet(dev(s, to_t, to_b))
        greet(dev(s, from_t, from_b))

    for p, g in steps:
        peer, there = neighbour(p, g)
        expected = expected + jnp.where(there, 1, 0)

        @pl.when(there)
        def _(peer=peer):
            greet(peer)

    pl.semaphore_wait(barrier, expected)

    pieces, piece_rows = tok.shape[2], tok.shape[3]
    planes = [b // 2, 2 + b // 2]

    def part(k):
        return tok_in.at[pl.ds(k * piece_rows, piece_rows)]

    def leg(i, k):
        return remote(
            part(k), relay.at[b % 2, k], z_send.at[i, k], z_recv.at[b % 2, k], dev(s, t, planes[i])
        )

    far_first = [1, 0]
    for i in far_first:

        @pl.when(planes[i] != b)
        def _(i=i):
            for k in range(pieces):
                leg(i, k).start()

    row_of = lax.broadcasted_iota(jnp.int32, lists_in.shape, 0)
    col_of = lax.broadcasted_iota(jnp.int32, lists_in.shape, 1)
    packed = jnp.zeros(lists_in.shape, jnp.int32)
    for i in range(tiles):
        for j in range(slots + 1):
            entry = ids[i, j] if j < slots else counts[i]
            packed = jnp.where((row_of == i) & (col_of == j), entry, packed)
    lists_in[...] = packed
    list_home = remote(lists_in, lists_v.at[e], l_send.at[0], l_recv.at[e], dev(s, from_t, from_b))
    list_away = remote(lists_in, lists_v.at[e], l_send.at[1], l_recv.at[e], dev(other, from_t, from_b))
    list_here = pltpu.make_async_copy(lists_in, lists_v.at[e], local.at[0])
    list_away.start()

    @pl.when(alone)
    def _():
        list_here.start()

    @pl.when(jnp.logical_not(alone))
    def _():
        list_home.start()

    u = jnp.where(c == 1, b, 3 - b)

    def at_u(where):
        return dev(s, t, jnp.where(c == 1, where, 3 - where))

    def slot(at):
        return jnp.where(c == 1, at, 3 - at)

    cuts = up_send.shape[1]
    cut_rows = w_in.shape[1] // cuts

    def cut(ref, r):
        return ref.at[pl.ds(r * cut_rows, cut_rows)]

    def own(h, r, where):
        target = 3 if where == 2 else 2
        return remote(
            cut(w_in.at[h], r), cut(w_all.at[h, b], r), up_send.at[h, r], w_recv.at[b, h, r], at_u(target)
        )

    def forward(h, r, at):
        place = cut(w_all.at[h, slot(at)], r)
        return remote(place, place, fwd_send.at[at, h, r], w_recv.at[slot(at), h, r], at_u(3))

    def across(src, h, r, at):
        place = cut(w_all.at[h, slot(at)], r)
        return remote(src, place, core_send.at[at, h, r], w_recv.at[slot(at), h, r], partner)

    def arrived(h, r, place):
        return remote(
            cut(w_in.at[h], r), cut(w_all.at[h, place], r), up_send.at[h, r], w_recv.at[place, h, r], partner
        )

    keep = pltpu.make_async_copy(w_in, w_all.at[:, b], local.at[1])

    def begin(where):
        for h in range(heads):
            for i in range(3):
                load(h, i).wait()
            for r in range(cuts):
                own(h, r, where).start()
                if where >= 2:
                    across(cut(w_in.at[h], r), h, r, where).start()
        if where >= 2:
            keep.start()

    for where in range(4):

        @pl.when(u == where)
        def _(where=where):
            begin(where)

    def spread(src, q, k):
        targets = [dev(s, 2 * couple + q, b), dev(other, 2 * couple + q, b)]
        targets += [dev(s, 2 * lax.rem(couple + j, couples) + q, b) for j in range(1, couples)]
        copies = [
            remote(src, tok.at[e, t, k], p_send.at[q, k, n], p_recv.at[e, t, k], peer)
            for n, peer in enumerate(targets)
        ]
        return copies, pltpu.make_async_copy(src, tok.at[e, t, k], local_t.at[k])

    def send(src, q, k):
        copies, here = spread(src, q, k)
        for copy in copies[1:]:
            copy.start()

        @pl.when(c == q)
        def _():
            here.start()

        @pl.when(c != q)
        def _():
            copies[0].start()

    def landed(from_e, from_t2, k):
        return remote(
            part(0), tok.at[from_e, from_t2, k], p_send.at[0, 0, 0], p_recv.at[from_e, from_t2, k], partner
        )

    def turn(n, k):
        if k % 2:
            from_t2 = 2 * lax.rem(couple + 1 + n // 2, couples) + n % 2
            return landed(e, from_t2, k), remote(
                tok.at[e, from_t2, k], tok.at[e, from_t2, k], turn_send.at[k, n],
                p_recv.at[e, from_t2, k], dev(other, t, b),
            )
        from_t2, jump = 2 * couple + n % 2, 1 + n // 2
        return landed(1 - e, from_t2, k), remote(
            tok.at[1 - e, from_t2, k], tok.at[1 - e, from_t2, k], turn_send.at[k, n],
            p_recv.at[1 - e, from_t2, k], dev(s, 2 * lax.rem(couple + jump, couples) + c, b),
        )

    turns = 2 * (couples - 1)
    for k in range(pieces):
        for n in range(2):
            q = jnp.where(b < 2, n, 1 - n)
            source = 2 * (b % 2) + q

            @pl.when(source == b)
            def _(q=q, k=k):
                send(part(k), q, k)

            @pl.when(source != b)
            def _(q=q, k=k):
                remote(part(k), relay.at[q, k], z_send.at[0, k], z_recv.at[q, k], partner).wait_recv()
                send(relay.at[q, k], q, k)

    def serve_2(h):
        for r in range(cuts):
            for at in (1, 0):
                arrived(h, r, slot(at)).wait_recv()
                forward(h, r, at).start()
                across(cut(w_all.at[h, slot(at)], r), h, r, at).start()
        for r in range(cuts):
            arrived(h, r, slot(3)).wait_recv()
            across(cut(w_all.at[h, slot(3)], r), h, r, 3).start()

    def serve(h):
        @pl.when(u == 3)
        def _():
            for r in range(cuts):
                for at in (2, 1, 0):
                    arrived(h, r, slot(at)).wait_recv()
                    across(cut(w_all.at[h, slot(at)], r), h, r, at).start()

        @pl.when(u < 2)
        def _():
            for r in range(cuts):
                for at in range(4):
                    arrived(h, r, at).wait_recv()

    def pass_on(k):
        for m in range(turns):
            here, on = turn(m, k)
            if k % 2 or m < 2:
                here.wait_recv()
            on.start()

    for h in range(heads - 1):
        for k in range(h * pieces // (heads - 1), (h + 1) * pieces // (heads - 1)):
            pass_on(k)

        @pl.when(u == 2)
        def _(h=h):
            serve_2(h)

    out_width = total.shape[1]

    def out_block(h, from_t2, half):
        place = pl.multiple_of((2 * from_t2 + half) * head_size, head_size)
        return w_cols.at[h, pl.ds(place, head_size)]

    def out_own(h, half):
        rows = pl.ds((half * heads + h) * head_size, head_size)
        src = w_out.at[rows, pl.ds(pl.multiple_of(t * out_width, out_width), out_width)]
        return pltpu.make_async_copy(src, out_block(h, t, half), o_local.at[h, half])

    partner_step = 1 - 2 * c

    def out_partner(h, half):
        target = t + partner_step
        rows = pl.ds((half * heads + h) * head_size, head_size)
        src = w_out.at[rows, pl.ds(pl.multiple_of(target * out_width, out_width), out_width)]
        return remote(src, out_block(h, t, half), o_send.at[0, h, half], o_recv.at[h, t, half], partner)

    def out_far(j, core, h):
        target = 2 * lax.rem(couple + j, couples) + core
        rows = pl.ds(pl.multiple_of((e * heads + h) * head_size, head_size), head_size)
        src = w_out.at[rows, pl.ds(pl.multiple_of(target * out_width, out_width), out_width)]
        return remote(
            src, out_block(h, t, e), o_send.at[2 * j + core, h, 0], o_recv.at[h, t, e], dev(s, target, b)
        )

    def out_turn(j, core, h):
        from_t2 = 2 * lax.rem(couple + j, couples) + core
        block = out_block(h, from_t2, e)
        return remote(
            block, block, o_send.at[2 * j + core, h, 1], o_recv.at[h, from_t2, e], dev(other, t, b)
        )

    def turn_columns(h):
        for j in range(1, couples):
            for core in range(2):
                on = out_turn(j, core, h)
                on.wait_recv()
                on.start()

    for h in range(heads):
        for j in range(1, couples):
            for core in range(2):
                out_far(j, core, h).start()
        for half in range(2):
            out_partner(h, half).start()
            out_own(h, half).start()

    remote(lists_in, lists_v.at[1 - e], l_send.at[0], l_recv.at[1 - e], partner).wait_recv()

    @pl.when(alone)
    def _():
        list_here.wait()

    @pl.when(jnp.logical_not(alone))
    def _():
        remote(lists_in, lists_v.at[e], l_send.at[0], l_recv.at[e], partner).wait_recv()

    down = pltpu.make_async_copy(lists_v, lists_s, local.at[3])
    down.start()
    down.wait()

    def set_places(tile, carry):
        half, i = tile // tiles, tile % tiles
        for j in range(slots):
            listed = lists_s[half, i, j]
            near = listed // (4 * tiles) - base
            group = jnp.where(near < 0, 2, jnp.where(near > 1, 3, near))
            row = listed // tiles % 4 - band_here + 1
            place = (row * groups + group) * tiles + listed % tiles
            place_s[tile, j] = jnp.clip(place, 0, 3 * groups * tiles - 1)
        place_s[tile, slots] = lists_s[half, i, slots]
        return carry

    lax.fori_loop(0, 2 * tiles, set_places, 0)

    block = 64 if piece_rows % 64 == 0 else piece_rows
    many = piece_rows // block

    def norm_piece(n, carry):
        half, k = lax.rem(e + n // pieces, 2), n % pieces

        @pl.when(half == e)
        def _():
            @pl.when(k % 2 == 0)
            def _():
                for j in range(2, tps):
                    landed(e, lax.rem(2 * couple + j, tps), k).wait_recv()

            landed(e, t + 1 - 2 * c, k).wait_recv()
            spread(part(0), c, k)[1].wait()

        @pl.when(half != e)
        def _():
            @pl.when(k % 2 == 1)
            def _():
                for j in range(2):
                    landed(1 - e, 2 * couple + j, k).wait_recv()

            for j in range(2, tps):
                landed(1 - e, lax.rem(2 * couple + j, tps), k).wait_recv()

        def norm_rows(i, inner):
            rows = pl.ds(pl.multiple_of(i * block, block), block)
            floats = jnp.concatenate([tok[half, j, k, rows, :] for j in range(tps)], axis=1).astype(F32)
            moved = floats - jnp.mean(floats, axis=-1, keepdims=True)
            spread_of = jnp.mean(moved * moved, axis=-1, keepdims=True)
            at = ((half * pieces + k) * many + i) * block
            normed[pl.ds(pl.multiple_of(at, block), block), :] = (
                moved * lax.rsqrt(spread_of + 1e-06) * (1.0 + scale[...]) + shift[...]
            ).astype(BF)
            return inner

        lax.fori_loop(0, many, norm_rows, 0)
        return carry

    lax.fori_loop(0, 2 * pieces, norm_piece, 0)

    @pl.when(u >= 2)
    def _():
        keep.wait()

    home = groups * tiles

    def multiplied(h, half, first, last):
        rows = pl.ds(pl.multiple_of(half * tok_rows, tok_rows), tok_rows)
        weights = w_all[h, :, :, first:last].reshape(normed.shape[1], last - first)
        return rows, jnp.dot(normed[rows, :], weights, preferred_element_type=F32)

    def project_keys(h):
        def rows_of(half, carry):
            _, product = multiplied(h, half, head_size, 3 * head_size)
            keys = head_norm(product[:, :head_size], k_gain[...])
            values = product[:, head_size:].astype(BF)
            for i in range(tiles):
                part = slice(i * tile_len, (i + 1) * tile_len)
                kvs[h][home + half * tiles + i, :, :head_size] = keys[part]
                kvs[h][home + half * tiles + i, :, head_size:] = values[part]
            return carry

        lax.fori_loop(0, 2, rows_of, 0)

    def project_queries(h):
        def rows_of(half, carry):
            rows, product = multiplied(h, half, 0, head_size)
            queries[h, rows, :] = head_norm(product, q_gain[...])
            return carry

        lax.fori_loop(0, 2, rows_of, 0)

    def share(h, n):
        p, g = steps[n]
        peer, there = neighbour(p, g)
        if p == 0:
            first, count, group = home, 2 * tiles, 0
        else:
            first, count, group = home + (tiles if p == 1 else 0), tiles, (2 if p == 1 else 3)
        target = (1 - g) * home + group * tiles
        copy = remote(
            kvs[h].at[pl.ds(first, count)], kvs[h].at[pl.ds(target, count)],
            kv_send.at[h, n], kv_recv.at[h, n], peer,
        )
        return copy, there

    def share_all(h):
        for n in range(len(steps)):
            copy, there = share(h, n)

            @pl.when(there)
            def _(copy=copy):
                copy.start()

    def shared(h):
        for n, (p, g) in enumerate(steps):
            copy, _ = share(h, n)
            _, there = neighbour(-p, -g)

            @pl.when(there)
            def _(copy=copy):
                copy.wait_recv()

    inverse = 1.0 / head_size**0.5
    pair = 2 * tile_len
    lane = lax.broadcasted_iota(jnp.int32, (1, pair), 1)

    def attend(h):
        kv = kvs[h]

        def near(tile, j, first):
            parts = []
            for i in range(2):
                at = place_s[tile, min(2 * j + i, slots - 1)]
                parts.append(kv[at, :, first : first + head_size])
            return jnp.concatenate(parts, axis=0)

        def tile_of(i, half):
            tile = half * tiles + i
            rows = pl.ds(pl.multiple_of(tile * tile_len, tile_len), tile_len)
            query = queries[h, rows, :]
            limit = place_s[tile, slots] * tile_len
            trips = (slots + 1) // 2
            top = None
            for j in range(trips):
                found = lax.dot_general(
                    query, near(tile, j, 0), (((1,), (1,)), ((), ())), preferred_element_type=F32
                )
                found = jnp.where(lane < limit - pair * j, found * inverse, -1e30)
                scores[half, :, j * pair : (j + 1) * pair] = found
                top = found if top is None else jnp.maximum(top, found)
            top = jnp.max(top, axis=-1, keepdims=True)
            total = None
            for j in range(trips):
                weights = jnp.exp(scores[half, :, j * pair : (j + 1) * pair] - top)
                scores[half, :, j * pair : (j + 1) * pair] = weights
                total = weights if total is None else total + weights
            part = 1.0 / jnp.sum(total, axis=-1, keepdims=True)
            result = None
            for j in range(trips):
                probs = (scores[half, :, j * pair : (j + 1) * pair] * part).astype(BF)
                found = jnp.dot(probs, near(tile, j, head_size), preferred_element_type=F32)
                result = found if result is None else result + found
            att[h, half, pl.ds(pl.multiple_of(i * tile_len, tile_len), tile_len), :] = result.astype(BF)

        def both(i, carry):
            tile_of(i, 0)
            tile_of(i, 1)
            return carry

        lax.fori_loop(0, tiles, both, 0)

    def deal(h):
        home_copy = remote(
            att.at[h, e], joint.at[h, 2 * to_t + e], j_send.at[h, 0], j_recv.at[h, e], dev(s, to_t, to_b)
        )
        here = pltpu.make_async_copy(att.at[h, e], joint.at[h, 2 * t + e], j_send.at[h, 0])
        away = remote(
            att.at[h, 1 - e], joint.at[h, 2 * to_t + e], j_send.at[h, 1], j_recv.at[h, e],
            dev(other, to_t, to_b),
        )
        return home_copy, here, away

    def start_deal(h):
        home_copy, here, away = deal(h)
        away.start()

        @pl.when(alone)
        def _():
            here.start()

        @pl.when(jnp.logical_not(alone))
        def _():
            home_copy.start()

    def hand(h, part_of, j):
        place = joint.at[h, 2 * t + part_of]
        peer = partner if j == 0 else dev(s, lax.rem(t + 2 * j, tps), b)
        return remote(place, place, a_send.at[h, part_of, j], a_recv.at[h, 2 * t + part_of], peer)

    def handed(h, from_t2, part_of):
        place = joint.at[h, 2 * from_t2 + part_of]
        return remote(
            place, place, r_send.at[h, part_of, from_t2 // 2], a_recv.at[h, 2 * from_t2 + part_of], partner
        )

    def hand_out(h):
        for m in range(2):
            part_of = e if m == 0 else 1 - e

            def arrive():
                remote(
                    att.at[h, 0], joint.at[h, 2 * t + part_of], j_send.at[h, 0], j_recv.at[h, part_of], partner
                ).wait_recv()

            if m == 0:

                @pl.when(alone)
                def _():
                    deal(h)[1].wait()

                @pl.when(jnp.logical_not(alone))
                def _():
                    arrive()
            else:
                arrive()
            for j in range(couples):
                hand(h, part_of, j).start()

    def multiply(h):
        for m in range(2):
            for j in range(1, couples):
                came = handed(h, lax.rem(t + 2 * j, tps), m)
                came.wait_recv()
                came.start()
        for m in range(2):
            handed(h, t + 1 - 2 * c, m).wait_recv()
            for j in range(1, couples):
                handed(h, lax.rem(t + 1 - 2 * c + 2 * j, tps), m).wait_recv()
        for half in range(2):
            out_own(h, half).wait()
            block = out_block(h, t + partner_step, half)
            remote(block, block, o_send.at[0, h, half], o_recv.at[h, t + partner_step, half], partner).wait_recv()
        for j in range(1, couples):
            for core in range(2):
                from_t2 = 2 * lax.rem(couple + j, couples) + core
                block = out_block(h, from_t2, 1 - e)
                remote(block, block, o_send.at[0, h, 0], o_recv.at[h, from_t2, 1 - e], partner).wait_recv()
        whole = jnp.concatenate([joint[h, i] for i in range(2 * tps)], axis=1)
        product = jnp.dot(whole, w_cols[h], preferred_element_type=F32)
        if h == 0:
            total[...] = product
        elif h < heads - 1:
            total[...] += product
        else:
            out[...] = total[...] + product

    last = heads - 1
    for h in range(last):
        serve(h)
        project_keys(h)
        share_all(h)
        project_queries(h)

    @pl.when(u == 2)
    def _():
        serve_2(last)

    for h in range(last):
        turn_columns(h)
        shared(h)
        attend(h)
        start_deal(h)
        if h:
            hand_out(h - 1)
    turn_columns(last)
    serve(last)
    project_keys(last)
    share_all(last)
    project_queries(last)
    hand_out(last - 1)
    for h in range(last - 1):
        multiply(h)
    shared(last)
    attend(last)
    start_deal(last)
    multiply(last - 1)
    hand_out(last)
    multiply(last)

    for where in range(4):

        @pl.when(u == where)
        def _(where=where):
            for h in range(heads):
                for r in range(cuts):
                    own(h, r, where).wait_send()
                    if where == 2:
                        for at in (1, 0):
                            forward(h, r, at).wait_send()
                    if where >= 2:
                        for at in range(4):
                            across(cut(w_in.at[h], r), h, r, at).wait_send()

    for i in range(2):

        @pl.when(planes[i] != b)
        def _(i=i):
            for k in range(pieces):
                leg(i, k).wait_send()

    for k in range(pieces):
        for q in range(2):
            copies, _ = spread(part(0), q, k)
            for copy in copies[1:]:
                copy.wait_send()

            @pl.when(c != q)
            def _(copy=copies[0]):
                copy.wait_send()

        for m in range(turns):
            turn(m, k)[1].wait_send()

    for h in range(heads):
        home_copy, _, away = deal(h)
        away.wait_send()

        @pl.when(jnp.logical_not(alone))
        def _(home_copy=home_copy):
            home_copy.wait_send()

        for j in range(1, couples):
            for core in range(2):
                out_far(j, core, h).wait_send()
                out_turn(j, core, h).wait_send()
        for m in range(2):
            for j in range(couples):
                hand(h, m, j).wait_send()
            for j in range(1, couples):
                handed(h, lax.rem(t + 2 * j, tps), m).wait_send()
            out_partner(h, m).wait_send()

    list_away.wait_send()

    @pl.when(jnp.logical_not(alone))
    def _():
        list_home.wait_send()

    for h in range(heads):
        for n in range(len(steps)):
            copy, there = share(h, n)

            @pl.when(there)
            def _(copy=copy):
                copy.wait_send()


def branch(tokens, w, scale, shift, q_gain, k_gain, ids, counts, w_out, slabs, tps):
    tok_rows, tok_width = tokens.shape
    tiles, slots = ids.shape
    head_size = q_gain.shape[0]
    heads, deep, wide = w.shape[2] // head_size // 2, w.shape[1], 3 * head_size
    tile_len = tok_rows // tiles
    width = scale.shape[0]
    pieces = 4 if tok_rows % 64 == 0 else 2
    cuts = 2
    groups = 4 if slabs > 2 else 2
    steps = 8 if slabs > 2 else 2
    dma = pltpu.SemaphoreType.DMA
    vmem = pl.BlockSpec(memory_space=pltpu.VMEM)
    smem = pl.BlockSpec(memory_space=pltpu.SMEM)
    lists = (8, 128)
    out_width = w_out.shape[1] // tps
    return pl.pallas_call(
        functools.partial(branch_kernel, (slabs, tps, heads, tiles, slots)),
        out_shape=jax.ShapeDtypeStruct((tok_rows, out_width), F32),
        in_specs=[vmem, pl.BlockSpec(memory_space=pl.ANY)] + [vmem] * 4 + [smem] * 2 + [pl.BlockSpec(memory_space=pl.ANY)],
        out_specs=vmem,
        scratch_shapes=[
            pltpu.VMEM(lists, jnp.int32),
            pltpu.VMEM((heads, deep, wide), BF),
            pltpu.VMEM((2, tps, pieces, tok_rows // pieces, tok_width), BF),
            pltpu.VMEM((heads, 4, deep, wide), BF),
            pltpu.VMEM((2, pieces, tok_rows // pieces, tok_width), BF),
            pltpu.VMEM((2 * tok_rows, width), BF),
            pltpu.VMEM((heads, 2 * tok_rows, head_size), BF),
            [pltpu.VMEM((3 * groups * tiles, tile_len, 2 * head_size), BF) for _ in range(heads)],
            pltpu.VMEM((heads, 2, tok_rows, head_size), BF),
            pltpu.VMEM((heads, 2 * tps, tok_rows, head_size), BF),
            pltpu.VMEM((heads, 2 * tps * head_size, out_width), BF),
            pltpu.VMEM((tok_rows, out_width), F32),
            pltpu.VMEM((2, tile_len, (slots + 1) // 2 * 2 * tile_len), F32),
            pltpu.VMEM((2,) + lists, jnp.int32),
            pltpu.SMEM((2,) + lists, jnp.int32),
            pltpu.SMEM((2 * tiles, slots + 1), jnp.int32),
            dma((2, pieces)), dma((2, pieces)), dma((2, pieces, tps)), dma((2, tps, pieces)),
            dma((pieces, tps)),
            dma((heads, cuts)), dma((2, heads, cuts)), dma((4, heads, cuts)), dma((4, heads, cuts)),
            dma((heads, steps)), dma((heads, steps)), dma((2,)), dma((2,)), dma((4,)), dma((pieces,)),
            dma((heads, 3)),
            dma((heads, 2)), dma((heads, 2)), dma((heads, 2, tps // 2)), dma((heads, 2 * tps)),
            dma((heads, 2, tps // 2)), dma((tps, heads, 2)), dma((heads, tps, 2)), dma((heads, 2)),
        ],
        compiler_params=pltpu.CompilerParams(
            collective_id=0, has_side_effects=True, vmem_limit_bytes=56 * 2**20
        ),
        name="branch",
    )(
        tokens, w, scale.reshape(1, -1), shift.reshape(1, -1), q_gain.reshape(1, -1),
        k_gain.reshape(1, -1), ids, counts, w_out,
    )


def shards(tokens, w_qkv, w_out, shift, scale, gate, q_gain, k_gain, tile_ids, key_counts):
    slabs, tps = lax.axis_size("slab"), lax.axis_size("tp")
    product = branch(
        tokens, w_qkv.transpose(1, 0, 2), scale, shift, q_gain, k_gain, tile_ids, key_counts, w_out,
        slabs, tps,
    )
    return (gate * product).astype(BF)


def solution(mesh):
    in_specs = (
        P(("slab", "band"), "tp"),
        P("band", None, "tp"),
        P("tp", None),
        P(),
        P(),
        P("tp"),
        P(),
        P(),
        P(("slab", "band"), None),
        P(("slab", "band")),
    )
    out_specs = P(("slab", "band"), "tp")
    return jax.shard_map(shards, mesh=mesh, in_specs=in_specs, out_specs=out_specs, check_vma=False)
```

```python
import functools

import jax
import jax.numpy as jnp
from jax import lax
from jax.experimental import pallas as pl
from jax.experimental.pallas import tpu as pltpu
from jax.sharding import PartitionSpec as P

BF = jnp.bfloat16
F32 = jnp.float32


def head_norm(piece, gain):
    squares = jnp.mean(piece * piece, axis=-1, keepdims=True)
    return (piece * lax.rsqrt(squares + 1e-06) * gain).astype(BF)


def branch_kernel(dims, tok_in, w_qkv, scale, shift, q_gain, k_gain, ids, counts, w_out, out, lists_in, w_in, tok, w_all,
                  relay, normed, queries, kvs, att, joint, w_cols, total, scores, lists_v, lists_s, place_s, z_send, z_recv, p_send,
                  p_recv, turn_send, up_send, fwd_send, core_send, w_recv, kv_send, kv_recv, l_send, l_recv,
                  local, local_t, w_sem,
                  j_send, j_recv, a_send, a_recv, r_send, o_send, o_recv, o_local):
    slabs, tps, heads, tiles, slots = dims
    s, t, b = lax.axis_index("slab"), lax.axis_index("tp"), lax.axis_index("band")
    e, c = s % 2, t % 2
    base = s - e
    couples, couple = tps // 2, t // 2
    kind = pl.DeviceIdType.MESH
    head_size = q_gain.shape[1]
    tok_rows, tok_width = tok_in.shape
    tile_len = tok_rows // tiles
    groups = 4 if slabs > 2 else 2
    band_here = 2 * (b % 2) + c
    alone = (c == b // 2) & (c == b % 2)
    other = s + 1 - 2 * e

    def dev(slab, tp, band):
        return {"slab": slab, "tp": tp, "band": band}

    def remote(src, dst, send, recv, peer):
        return pltpu.make_async_remote_copy(src, dst, send, recv, device_id=peer, device_id_type=kind)

    to_t, to_b = 2 * couple + b // 2, 2 * (b % 2) + c
    from_t, from_b = 2 * couple + b % 2, 2 * c + b // 2
    partner = dev(s, t + 1 - 2 * c, b)

    steps = [(0, 1), (0, -1)]
    if slabs > 2:
        steps += [(p, g) for p in (1, -1) for g in (0, 1, -1)]

    def neighbour(p, g):
        at = band_here + g
        there = (at >= 0) & (at <= 3)
        if p:
            there = there & (s + 2 * p >= 0) & (s + 2 * p < slabs)
        at = jnp.clip(at, 0, 3)
        slab = jnp.clip(s + 2 * p, 0, slabs - 1) if p else s
        return dev(slab, 2 * couple + at % 2, 2 * (b // 2) + at // 2), there

    def load(h, i):
        first = pl.multiple_of(e * heads * head_size + h * head_size, head_size)
        cols = slice(i * head_size, (i + 1) * head_size)
        return pltpu.make_async_copy(
            w_qkv.at[i, :, pl.ds(first, head_size)], w_in.at[h, :, cols], w_sem.at[h, i]
        )

    for h in range(heads):
        for i in range(3):
            load(h, i).start()

    barrier = pltpu.get_barrier_semaphore()

    def greet(peer):
        pl.semaphore_signal(barrier, inc=1, device_id=peer, device_id_type=kind)

    peers = [dev(s, t, (b + i) % 4) for i in range(1, 4)]
    for i in range(2):
        for j in range(tps):
            if i or j:
                peers.append(dev(base + (e + i) % 2, (t + j) % tps, b))
    peers += [dev(other, to_t, to_b), dev(other, from_t, from_b)]
    for peer in peers:
        greet(peer)
    expected = len(peers) + jnp.where(alone, 0, 2)

    @pl.when(jnp.logical_not(alone))
    def _():
        greet(dev(s, to_t, to_b))
        greet(dev(s, from_t, from_b))

    for p, g in steps:
        peer, there = neighbour(p, g)
        expected = expected + jnp.where(there, 1, 0)

        @pl.when(there)
        def _(peer=peer):
            greet(peer)

    pl.semaphore_wait(barrier, expected)

    pieces, piece_rows = tok.shape[2], tok.shape[3]
    planes = [b // 2, 2 + b // 2]

    def part(k):
        return tok_in.at[pl.ds(k * piece_rows, piece_rows)]

    def leg(i, k):
        return remote(
            part(k), relay.at[b % 2, k], z_send.at[i, k], z_recv.at[b % 2, k], dev(s, t, planes[i])
        )

    far_first = [1, 0]
    for i in far_first:

        @pl.when(planes[i] != b)
        def _(i=i):
            for k in range(pieces):
                leg(i, k).start()

    row_of = lax.broadcasted_iota(jnp.int32, lists_in.shape, 0)
    col_of = lax.broadcasted_iota(jnp.int32, lists_in.shape, 1)
    packed = jnp.zeros(lists_in.shape, jnp.int32)
    for i in range(tiles):
        for j in range(slots + 1):
            entry = ids[i, j] if j < slots else counts[i]
            packed = jnp.where((row_of == i) & (col_of == j), entry, packed)
    lists_in[...] = packed
    list_home = remote(lists_in, lists_v.at[e], l_send.at[0], l_recv.at[e], dev(s, from_t, from_b))
    list_away = remote(lists_in, lists_v.at[e], l_send.at[1], l_recv.at[e], dev(other, from_t, from_b))
    list_here = pltpu.make_async_copy(lists_in, lists_v.at[e], local.at[0])
    list_away.start()

    @pl.when(alone)
    def _():
        list_here.start()

    @pl.when(jnp.logical_not(alone))
    def _():
        list_home.start()

    u = jnp.where(c == 1, b, 3 - b)

    def at_u(where):
        return dev(s, t, jnp.where(c == 1, where, 3 - where))

    def slot(at):
        return jnp.where(c == 1, at, 3 - at)

    cuts = up_send.shape[1]

    def cut(ref, r):
        return ref.at[:, pl.ds(0, head_size)] if r else ref.at[:, pl.ds(head_size, 2 * head_size)]

    def own(h, r, where):
        target = 3 if where == 2 else 2
        return remote(
            cut(w_in.at[h], r), cut(w_all.at[h, b], r), up_send.at[h, r], w_recv.at[b, h, r], at_u(target)
        )

    def forward(h, r, at):
        place = cut(w_all.at[h, slot(at)], r)
        return remote(place, place, fwd_send.at[at, h, r], w_recv.at[slot(at), h, r], at_u(3))

    def across(src, h, r, at):
        place = cut(w_all.at[h, slot(at)], r)
        return remote(src, place, core_send.at[at, h, r], w_recv.at[slot(at), h, r], partner)

    def arrived(h, r, place):
        return remote(
            cut(w_in.at[h], r), cut(w_all.at[h, place], r), up_send.at[h, r], w_recv.at[place, h, r], partner
        )

    keep = pltpu.make_async_copy(w_in, w_all.at[:, b], local.at[1])

    def begin(where):
        for h in range(heads):
            for i in range(3):
                load(h, i).wait()
            for r in range(cuts):
                own(h, r, where).start()
                if where >= 2:
                    across(cut(w_in.at[h], r), h, r, where).start()
        if where >= 2:
            keep.start()

    for where in range(4):

        @pl.when(u == where)
        def _(where=where):
            begin(where)

    def spread(src, q, k):
        targets = [dev(s, 2 * couple + q, b), dev(other, 2 * couple + q, b)]
        targets += [dev(s, 2 * lax.rem(couple + j, couples) + q, b) for j in range(1, couples)]
        copies = [
            remote(src, tok.at[e, t, k], p_send.at[q, k, n], p_recv.at[e, t, k], peer)
            for n, peer in enumerate(targets)
        ]
        return copies, pltpu.make_async_copy(src, tok.at[e, t, k], local_t.at[k])

    def send(src, q, k):
        copies, here = spread(src, q, k)
        for copy in copies[1:]:
            copy.start()

        @pl.when(c == q)
        def _():
            here.start()

        @pl.when(c != q)
        def _():
            copies[0].start()

    def landed(from_e, from_t2, k):
        return remote(
            part(0), tok.at[from_e, from_t2, k], p_send.at[0, 0, 0], p_recv.at[from_e, from_t2, k], partner
        )

    def turn(n, k):
        if k % 2:
            from_t2 = 2 * lax.rem(couple + 1 + n // 2, couples) + n % 2
            return landed(e, from_t2, k), remote(
                tok.at[e, from_t2, k], tok.at[e, from_t2, k], turn_send.at[k, n],
                p_recv.at[e, from_t2, k], dev(other, t, b),
            )
        from_t2, jump = 2 * couple + n % 2, 1 + n // 2
        return landed(1 - e, from_t2, k), remote(
            tok.at[1 - e, from_t2, k], tok.at[1 - e, from_t2, k], turn_send.at[k, n],
            p_recv.at[1 - e, from_t2, k], dev(s, 2 * lax.rem(couple + jump, couples) + c, b),
        )

    turns = 2 * (couples - 1)
    for k in range(pieces):
        for n in range(2):
            q = jnp.where(b < 2, n, 1 - n)
            source = 2 * (b % 2) + q

            @pl.when(source == b)
            def _(q=q, k=k):
                send(part(k), q, k)

            @pl.when(source != b)
            def _(q=q, k=k):
                remote(part(k), relay.at[q, k], z_send.at[0, k], z_recv.at[q, k], partner).wait_recv()
                send(relay.at[q, k], q, k)

    def serve_2(h, r):
        for at in (1, 0):
            arrived(h, r, slot(at)).wait_recv()
            forward(h, r, at).start()
            across(cut(w_all.at[h, slot(at)], r), h, r, at).start()
        arrived(h, r, slot(3)).wait_recv()
        across(cut(w_all.at[h, slot(3)], r), h, r, 3).start()

    def serve(h, r):
        @pl.when(u == 3)
        def _():
            for at in (2, 1, 0):
                arrived(h, r, slot(at)).wait_recv()
                across(cut(w_all.at[h, slot(at)], r), h, r, at).start()

        @pl.when(u < 2)
        def _():
            for at in range(4):
                arrived(h, r, at).wait_recv()

    def pass_on(k):
        for m in range(turns):
            here, on = turn(m, k)
            if k % 2 or m < 2:
                here.wait_recv()
            on.start()

    for h in range(heads - 1):
        for k in range(h * pieces // (heads - 1), (h + 1) * pieces // (heads - 1)):
            pass_on(k)

        @pl.when(u == 2)
        def _(h=h):
            for r in range(cuts):
                serve_2(h, r)

    out_width = total.shape[1]

    def out_block(h, from_t2, half):
        place = pl.multiple_of((2 * from_t2 + half) * head_size, head_size)
        return w_cols.at[h, pl.ds(place, head_size)]

    def out_own(h, half):
        rows = pl.ds((half * heads + h) * head_size, head_size)
        src = w_out.at[rows, pl.ds(pl.multiple_of(t * out_width, out_width), out_width)]
        return pltpu.make_async_copy(src, out_block(h, t, half), o_local.at[h, half])

    partner_step = 1 - 2 * c

    def out_partner(h, half):
        target = t + partner_step
        rows = pl.ds((half * heads + h) * head_size, head_size)
        src = w_out.at[rows, pl.ds(pl.multiple_of(target * out_width, out_width), out_width)]
        return remote(src, out_block(h, t, half), o_send.at[0, h, half], o_recv.at[h, t, half], partner)

    def out_far(j, core, h):
        target = 2 * lax.rem(couple + j, couples) + core
        rows = pl.ds(pl.multiple_of((e * heads + h) * head_size, head_size), head_size)
        src = w_out.at[rows, pl.ds(pl.multiple_of(target * out_width, out_width), out_width)]
        return remote(
            src, out_block(h, t, e), o_send.at[2 * j + core, h, 0], o_recv.at[h, t, e], dev(s, target, b)
        )

    def out_turn(j, core, h):
        from_t2 = 2 * lax.rem(couple + j, couples) + core
        block = out_block(h, from_t2, e)
        return remote(
            block, block, o_send.at[2 * j + core, h, 1], o_recv.at[h, from_t2, e], dev(other, t, b)
        )

    def turn_columns(h):
        for j in range(1, couples):
            for core in range(2):
                on = out_turn(j, core, h)
                on.wait_recv()
                on.start()

    for h in range(heads):
        for j in range(1, couples):
            for core in range(2):
                out_far(j, core, h).start()
        for half in range(2):
            out_partner(h, half).start()
            out_own(h, half).start()

    remote(lists_in, lists_v.at[1 - e], l_send.at[0], l_recv.at[1 - e], partner).wait_recv()

    @pl.when(alone)
    def _():
        list_here.wait()

    @pl.when(jnp.logical_not(alone))
    def _():
        remote(lists_in, lists_v.at[e], l_send.at[0], l_recv.at[e], partner).wait_recv()

    down = pltpu.make_async_copy(lists_v, lists_s, local.at[3])
    down.start()
    down.wait()

    def set_places(tile, carry):
        half, i = tile // tiles, tile % tiles
        for j in range(slots):
            listed = lists_s[half, i, j]
            near = listed // (4 * tiles) - base
            group = jnp.where(near < 0, 2, jnp.where(near > 1, 3, near))
            row = listed // tiles % 4 - band_here + 1
            place = (row * groups + group) * tiles + listed % tiles
            place_s[tile, j] = jnp.clip(place, 0, 3 * groups * tiles - 1)
        place_s[tile, slots] = lists_s[half, i, slots]
        return carry

    lax.fori_loop(0, 2 * tiles, set_places, 0)

    block = 64 if piece_rows % 64 == 0 else piece_rows
    many = piece_rows // block

    def norm_piece(n, carry):
        half, k = lax.rem(e + n // pieces, 2), n % pieces

        @pl.when(half == e)
        def _():
            @pl.when(k % 2 == 0)
            def _():
                for j in range(2, tps):
                    landed(e, lax.rem(2 * couple + j, tps), k).wait_recv()

            landed(e, t + 1 - 2 * c, k).wait_recv()
            spread(part(0), c, k)[1].wait()

        @pl.when(half != e)
        def _():
            @pl.when(k % 2 == 1)
            def _():
                for j in range(2):
                    landed(1 - e, 2 * couple + j, k).wait_recv()

            for j in range(2, tps):
                landed(1 - e, lax.rem(2 * couple + j, tps), k).wait_recv()

        def norm_rows(i, inner):
            rows = pl.ds(pl.multiple_of(i * block, block), block)
            floats = jnp.concatenate([tok[half, j, k, rows, :] for j in range(tps)], axis=1).astype(F32)
            moved = floats - jnp.mean(floats, axis=-1, keepdims=True)
            spread_of = jnp.mean(moved * moved, axis=-1, keepdims=True)
            at = ((half * pieces + k) * many + i) * block
            normed[pl.ds(pl.multiple_of(at, block), block), :] = (
                moved * lax.rsqrt(spread_of + 1e-06) * (1.0 + scale[...]) + shift[...]
            ).astype(BF)
            return inner

        lax.fori_loop(0, many, norm_rows, 0)
        return carry

    lax.fori_loop(0, 2 * pieces, norm_piece, 0)

    @pl.when(u >= 2)
    def _():
        keep.wait()

    home = groups * tiles

    def multiplied(h, half, first, last):
        rows = pl.ds(pl.multiple_of(half * tok_rows, tok_rows), tok_rows)
        weights = w_all[h, :, :, first:last].reshape(normed.shape[1], last - first)
        return rows, jnp.dot(normed[rows, :], weights, preferred_element_type=F32)

    def project_keys(h):
        def rows_of(half, carry):
            _, product = multiplied(h, half, head_size, 3 * head_size)
            keys = head_norm(product[:, :head_size], k_gain[...])
            values = product[:, head_size:].astype(BF)
            for i in range(tiles):
                part = slice(i * tile_len, (i + 1) * tile_len)
                kvs[h][home + half * tiles + i, :, :head_size] = keys[part]
                kvs[h][home + half * tiles + i, :, head_size:] = values[part]
            return carry

        lax.fori_loop(0, 2, rows_of, 0)

    def project_queries(h):
        def rows_of(half, carry):
            rows, product = multiplied(h, half, 0, head_size)
            queries[h, rows, :] = head_norm(product, q_gain[...])
            return carry

        lax.fori_loop(0, 2, rows_of, 0)

    def share(h, n):
        p, g = steps[n]
        peer, there = neighbour(p, g)
        if p == 0:
            first, count, group = home, 2 * tiles, 0
        else:
            first, count, group = home + (tiles if p == 1 else 0), tiles, (2 if p == 1 else 3)
        target = (1 - g) * home + group * tiles
        copy = remote(
            kvs[h].at[pl.ds(first, count)], kvs[h].at[pl.ds(target, count)],
            kv_send.at[h, n], kv_recv.at[h, n], peer,
        )
        return copy, there

    def share_all(h):
        for n in range(len(steps)):
            copy, there = share(h, n)

            @pl.when(there)
            def _(copy=copy):
                copy.start()

    def shared(h):
        for n, (p, g) in enumerate(steps):
            copy, _ = share(h, n)
            _, there = neighbour(-p, -g)

            @pl.when(there)
            def _(copy=copy):
                copy.wait_recv()

    def tile_rows(i):
        return pl.ds(i * tile_len if isinstance(i, int) else pl.multiple_of(i * tile_len, tile_len), tile_len)

    def deal(h, i):
        rows = tile_rows(i)
        place = joint.at[h, 2 * to_t + e, rows]
        home_copy = remote(att.at[h, e, rows], place, j_send.at[h, 0, i], j_recv.at[h, e, i], dev(s, to_t, to_b))
        here = pltpu.make_async_copy(att.at[h, e, rows], joint.at[h, 2 * t + e, rows], j_send.at[h, 0, i])
        away = remote(
            att.at[h, 1 - e, rows], place, j_send.at[h, 1, i], j_recv.at[h, e, i], dev(other, to_t, to_b)
        )
        return home_copy, here, away

    def start_deal(h, i):
        home_copy, here, away = deal(h, i)
        away.start()

        @pl.when(alone)
        def _():
            here.start()

        @pl.when(jnp.logical_not(alone))
        def _():
            home_copy.start()

    inverse = 1.0 / head_size**0.5
    pair = 2 * tile_len
    lane = lax.broadcasted_iota(jnp.int32, (1, pair), 1)

    def attend(h):
        kv = kvs[h]

        def near(tile, j, first):
            parts = []
            for i in range(2):
                at = place_s[tile, min(2 * j + i, slots - 1)]
                parts.append(kv[at, :, first : first + head_size])
            return jnp.concatenate(parts, axis=0)

        def tile_of(i, half):
            tile = half * tiles + i
            rows = pl.ds(pl.multiple_of(tile * tile_len, tile_len), tile_len)
            query = queries[h, rows, :]
            limit = place_s[tile, slots] * tile_len
            trips = (slots + 1) // 2
            top = None
            for j in range(trips):
                found = lax.dot_general(
                    query, near(tile, j, 0), (((1,), (1,)), ((), ())), preferred_element_type=F32
                )
                found = jnp.where(lane < limit - pair * j, found * inverse, -1e30)
                scores[half, :, j * pair : (j + 1) * pair] = found
                top = found if top is None else jnp.maximum(top, found)
            top = jnp.max(top, axis=-1, keepdims=True)
            total = None
            for j in range(trips):
                weights = jnp.exp(scores[half, :, j * pair : (j + 1) * pair] - top)
                scores[half, :, j * pair : (j + 1) * pair] = weights
                total = weights if total is None else total + weights
            part = 1.0 / jnp.sum(total, axis=-1, keepdims=True)
            result = None
            for j in range(trips):
                probs = (scores[half, :, j * pair : (j + 1) * pair] * part).astype(BF)
                found = jnp.dot(probs, near(tile, j, head_size), preferred_element_type=F32)
                result = found if result is None else result + found
            att[h, half, pl.ds(pl.multiple_of(i * tile_len, tile_len), tile_len), :] = result.astype(BF)

        def both(i, carry):
            tile_of(i, 0)
            tile_of(i, 1)
            start_deal(h, i)
            return carry

        lax.fori_loop(0, tiles, both, 0)

    def hand(h, part_of, i, j):
        place = joint.at[h, 2 * t + part_of, tile_rows(i)]
        peer = partner if j == 0 else dev(s, lax.rem(t + 2 * j, tps), b)
        return remote(place, place, a_send.at[h, part_of, i, j], a_recv.at[h, 2 * t + part_of, i], peer)

    def handed(h, from_t2, part_of, i):
        place = joint.at[h, 2 * from_t2 + part_of, tile_rows(i)]
        return remote(
            place, place, r_send.at[h, part_of, i, from_t2 // 2], a_recv.at[h, 2 * from_t2 + part_of, i], partner
        )

    def hand_out(h):
        for i in range(tiles):
            for m in range(2):
                part_of = e if m == 0 else 1 - e

                def arrive():
                    place = joint.at[h, 2 * t + part_of, tile_rows(i)]
                    remote(place, place, j_send.at[h, 0, i], j_recv.at[h, part_of, i], partner).wait_recv()

                if m == 0:

                    @pl.when(alone)
                    def _():
                        deal(h, i)[1].wait()

                    @pl.when(jnp.logical_not(alone))
                    def _():
                        arrive()
                else:
                    arrive()
                for j in range(1, couples):
                    hand(h, part_of, i, j).start()
                hand(h, part_of, i, 0).start()

    def multiply(h):
        for i in range(tiles):
            for m in range(2):
                for j in range(1, couples):
                    came = handed(h, lax.rem(t + 2 * j, tps), m, i)
                    came.wait_recv()
                    came.start()
        for i in range(tiles):
            for m in range(2):
                for j in range(couples):
                    handed(h, lax.rem(t + 1 - 2 * c + 2 * j, tps), m, i).wait_recv()
        for half in range(2):
            out_own(h, half).wait()
            block = out_block(h, t + partner_step, half)
            remote(block, block, o_send.at[0, h, half], o_recv.at[h, t + partner_step, half], partner).wait_recv()
        for j in range(1, couples):
            for core in range(2):
                from_t2 = 2 * lax.rem(couple + j, couples) + core
                block = out_block(h, from_t2, 1 - e)
                remote(block, block, o_send.at[0, h, 0], o_recv.at[h, from_t2, 1 - e], partner).wait_recv()
        whole = jnp.concatenate([joint[h, i] for i in range(2 * tps)], axis=1)
        product = jnp.dot(whole, w_cols[h], preferred_element_type=F32)
        if h == 0:
            total[...] = product
        elif h < heads - 1:
            total[...] += product
        else:
            out[...] = total[...] + product

    last = heads - 1

    def project(h):
        serve(h, 0)
        project_keys(h)
        share_all(h)
        serve(h, 1)
        project_queries(h)

    for h in range(last):
        project(h)

    @pl.when(u == 2)
    def _():
        for r in range(cuts):
            serve_2(last, r)

    for h in range(last):
        turn_columns(h)
        shared(h)
        attend(h)
        if h:
            hand_out(h - 1)
    turn_columns(last)
    project(last)
    hand_out(last - 1)
    for h in range(last - 1):
        multiply(h)
    shared(last)
    attend(last)
    hand_out(last)
    multiply(last - 1)
    multiply(last)

    for where in range(4):

        @pl.when(u == where)
        def _(where=where):
            for h in range(heads):
                for r in range(cuts):
                    own(h, r, where).wait_send()
                    if where == 2:
                        for at in (1, 0):
                            forward(h, r, at).wait_send()
                    if where >= 2:
                        for at in range(4):
                            across(cut(w_in.at[h], r), h, r, at).wait_send()

    for i in range(2):

        @pl.when(planes[i] != b)
        def _(i=i):
            for k in range(pieces):
                leg(i, k).wait_send()

    for k in range(pieces):
        for q in range(2):
            copies, _ = spread(part(0), q, k)
            for copy in copies[1:]:
                copy.wait_send()

            @pl.when(c != q)
            def _(copy=copies[0]):
                copy.wait_send()

        for m in range(turns):
            turn(m, k)[1].wait_send()

    for h in range(heads):
        for i in range(tiles):
            home_copy, _, away = deal(h, i)
            away.wait_send()

            @pl.when(jnp.logical_not(alone))
            def _(home_copy=home_copy):
                home_copy.wait_send()

            for m in range(2):
                for j in range(couples):
                    hand(h, m, i, j).wait_send()
                for j in range(1, couples):
                    handed(h, lax.rem(t + 2 * j, tps), m, i).wait_send()

        for j in range(1, couples):
            for core in range(2):
                out_far(j, core, h).wait_send()
                out_turn(j, core, h).wait_send()
        for m in range(2):
            out_partner(h, m).wait_send()

    list_away.wait_send()

    @pl.when(jnp.logical_not(alone))
    def _():
        list_home.wait_send()

    for h in range(heads):
        for n in range(len(steps)):
            copy, there = share(h, n)

            @pl.when(there)
            def _(copy=copy):
                copy.wait_send()


def branch(tokens, w, scale, shift, q_gain, k_gain, ids, counts, w_out, slabs, tps):
    tok_rows, tok_width = tokens.shape
    tiles, slots = ids.shape
    head_size = q_gain.shape[0]
    heads, deep, wide = w.shape[2] // head_size // 2, w.shape[1], 3 * head_size
    tile_len = tok_rows // tiles
    width = scale.shape[0]
    pieces = 4 if tok_rows % 64 == 0 else 2
    cuts = 2
    groups = 4 if slabs > 2 else 2
    steps = 8 if slabs > 2 else 2
    dma = pltpu.SemaphoreType.DMA
    vmem = pl.BlockSpec(memory_space=pltpu.VMEM)
    smem = pl.BlockSpec(memory_space=pltpu.SMEM)
    lists = (8, 128)
    out_width = w_out.shape[1] // tps
    return pl.pallas_call(
        functools.partial(branch_kernel, (slabs, tps, heads, tiles, slots)),
        out_shape=jax.ShapeDtypeStruct((tok_rows, out_width), F32),
        in_specs=[vmem, pl.BlockSpec(memory_space=pl.ANY)] + [vmem] * 4 + [smem] * 2 + [pl.BlockSpec(memory_space=pl.ANY)],
        out_specs=vmem,
        scratch_shapes=[
            pltpu.VMEM(lists, jnp.int32),
            pltpu.VMEM((heads, deep, wide), BF),
            pltpu.VMEM((2, tps, pieces, tok_rows // pieces, tok_width), BF),
            pltpu.VMEM((heads, 4, deep, wide), BF),
            pltpu.VMEM((2, pieces, tok_rows // pieces, tok_width), BF),
            pltpu.VMEM((2 * tok_rows, width), BF),
            pltpu.VMEM((heads, 2 * tok_rows, head_size), BF),
            [pltpu.VMEM((3 * groups * tiles, tile_len, 2 * head_size), BF) for _ in range(heads)],
            pltpu.VMEM((heads, 2, tok_rows, head_size), BF),
            pltpu.VMEM((heads, 2 * tps, tok_rows, head_size), BF),
            pltpu.VMEM((heads, 2 * tps * head_size, out_width), BF),
            pltpu.VMEM((tok_rows, out_width), F32),
            pltpu.VMEM((2, tile_len, (slots + 1) // 2 * 2 * tile_len), F32),
            pltpu.VMEM((2,) + lists, jnp.int32),
            pltpu.SMEM((2,) + lists, jnp.int32),
            pltpu.SMEM((2 * tiles, slots + 1), jnp.int32),
            dma((2, pieces)), dma((2, pieces)), dma((2, pieces, tps)), dma((2, tps, pieces)),
            dma((pieces, tps)),
            dma((heads, cuts)), dma((2, heads, cuts)), dma((4, heads, cuts)), dma((4, heads, cuts)),
            dma((heads, steps)), dma((heads, steps)), dma((2,)), dma((2,)), dma((4,)), dma((pieces,)),
            dma((heads, 3)),
            dma((heads, 2, tiles)), dma((heads, 2, tiles)), dma((heads, 2, tiles, tps // 2)),
            dma((heads, 2 * tps, tiles)), dma((heads, 2, tiles, tps // 2)), dma((tps, heads, 2)), dma((heads, tps, 2)), dma((heads, 2)),
        ],
        compiler_params=pltpu.CompilerParams(
            collective_id=0, has_side_effects=True, vmem_limit_bytes=56 * 2**20
        ),
        name="branch",
    )(
        tokens, w, scale.reshape(1, -1), shift.reshape(1, -1), q_gain.reshape(1, -1),
        k_gain.reshape(1, -1), ids, counts, w_out,
    )


def shards(tokens, w_qkv, w_out, shift, scale, gate, q_gain, k_gain, tile_ids, key_counts):
    slabs, tps = lax.axis_size("slab"), lax.axis_size("tp")
    product = branch(
        tokens, w_qkv.transpose(1, 0, 2), scale, shift, q_gain, k_gain, tile_ids, key_counts, w_out,
        slabs, tps,
    )
    return (gate * product).astype(BF)


def solution(mesh):
    in_specs = (
        P(("slab", "band"), "tp"),
        P("band", None, "tp"),
        P("tp", None),
        P(),
        P(),
        P("tp"),
        P(),
        P(),
        P(("slab", "band"), None),
        P(("slab", "band")),
    )
    out_specs = P(("slab", "band"), "tp")
    return jax.shard_map(shards, mesh=mesh, in_specs=in_specs, out_specs=out_specs, check_vma=False)
```

```python
import functools

import jax
import jax.numpy as jnp
from jax import lax
from jax.experimental import pallas as pl
from jax.experimental.pallas import tpu as pltpu
from jax.sharding import PartitionSpec as P

BF = jnp.bfloat16
F32 = jnp.float32


def head_norm(piece, gain):
    squares = jnp.mean(piece * piece, axis=-1, keepdims=True)
    return (piece * lax.rsqrt(squares + 1e-06) * gain).astype(BF)


def branch_kernel(dims, tok_in, w_qkv, scale, shift, q_gain, k_gain, ids, counts, w_out, out, lists_in, w_in, tok, w_all,
                  relay, normed, queries, kvs, att, joint, w_cols, total, scores, lists_v, lists_s, place_s, z_send, z_recv, p_send,
                  p_recv, turn_send, up_send, fwd_send, core_send, w_recv, kv_send, kv_recv, l_send, l_recv,
                  local, local_t, w_sem,
                  j_send, j_recv, a_send, a_recv, r_send, o_send, o_recv, o_local):
    slabs, tps, heads, tiles, slots = dims
    s, t, b = lax.axis_index("slab"), lax.axis_index("tp"), lax.axis_index("band")
    e, c = s % 2, t % 2
    base = s - e
    couples, couple = tps // 2, t // 2
    kind = pl.DeviceIdType.MESH
    head_size = q_gain.shape[1]
    tok_rows, tok_width = tok_in.shape
    tile_len = tok_rows // tiles
    groups = 4 if slabs > 2 else 2
    band_here = 2 * (b % 2) + c
    alone = (c == b // 2) & (c == b % 2)
    other = s + 1 - 2 * e

    def dev(slab, tp, band):
        return {"slab": slab, "tp": tp, "band": band}

    def remote(src, dst, send, recv, peer):
        return pltpu.make_async_remote_copy(src, dst, send, recv, device_id=peer, device_id_type=kind)

    to_t, to_b = 2 * couple + b // 2, 2 * (b % 2) + c
    from_t, from_b = 2 * couple + b % 2, 2 * c + b // 2
    partner = dev(s, t + 1 - 2 * c, b)

    steps = [(0, 1), (0, -1)]
    if slabs > 2:
        steps += [(p, g) for p in (1, -1) for g in (0, 1, -1)]

    def neighbour(p, g):
        at = band_here + g
        there = (at >= 0) & (at <= 3)
        if p:
            there = there & (s + 2 * p >= 0) & (s + 2 * p < slabs)
        at = jnp.clip(at, 0, 3)
        slab = jnp.clip(s + 2 * p, 0, slabs - 1) if p else s
        return dev(slab, 2 * couple + at % 2, 2 * (b // 2) + at // 2), there

    def load(h, i):
        first = pl.multiple_of(e * heads * head_size + h * head_size, head_size)
        cols = slice(i * head_size, (i + 1) * head_size)
        return pltpu.make_async_copy(
            w_qkv.at[i, :, pl.ds(first, head_size)], w_in.at[h, :, cols], w_sem.at[h, i]
        )

    barrier = pltpu.get_barrier_semaphore()

    def greet(peer):
        pl.semaphore_signal(barrier, inc=1, device_id=peer, device_id_type=kind)

    peers = [dev(s, t, (b + i) % 4) for i in range(1, 4)]
    for i in range(2):
        for j in range(tps):
            if i or j:
                peers.append(dev(base + (e + i) % 2, (t + j) % tps, b))
    peers += [dev(other, to_t, to_b), dev(other, from_t, from_b)]
    for peer in peers:
        greet(peer)
    expected = len(peers) + jnp.where(alone, 0, 2)

    @pl.when(jnp.logical_not(alone))
    def _():
        greet(dev(s, to_t, to_b))
        greet(dev(s, from_t, from_b))

    for p, g in steps:
        peer, there = neighbour(p, g)
        expected = expected + jnp.where(there, 1, 0)

        @pl.when(there)
        def _(peer=peer):
            greet(peer)

    for h in range(heads):
        for i in range(3):
            load(h, i).start()

    pl.semaphore_wait(barrier, expected)

    pieces, piece_rows = tok.shape[2], tok.shape[3]
    planes = [b // 2, 2 + b // 2]

    def part(k):
        return tok_in.at[pl.ds(k * piece_rows, piece_rows)]

    def leg(i, k):
        return remote(
            part(k), relay.at[b % 2, k], z_send.at[i, k], z_recv.at[b % 2, k], dev(s, t, planes[i])
        )

    far_first = [1, 0]
    for i in far_first:

        @pl.when(planes[i] != b)
        def _(i=i):
            for k in range(pieces):
                leg(i, k).start()

    row_of = lax.broadcasted_iota(jnp.int32, lists_in.shape, 0)
    col_of = lax.broadcasted_iota(jnp.int32, lists_in.shape, 1)
    packed = jnp.zeros(lists_in.shape, jnp.int32)
    for i in range(tiles):
        for j in range(slots + 1):
            entry = ids[i, j] if j < slots else counts[i]
            packed = jnp.where((row_of == i) & (col_of == j), entry, packed)
    lists_in[...] = packed
    list_home = remote(lists_in, lists_v.at[e], l_send.at[0], l_recv.at[e], dev(s, from_t, from_b))
    list_away = remote(lists_in, lists_v.at[e], l_send.at[1], l_recv.at[e], dev(other, from_t, from_b))
    list_here = pltpu.make_async_copy(lists_in, lists_v.at[e], local.at[0])
    list_away.start()

    @pl.when(alone)
    def _():
        list_here.start()

    @pl.when(jnp.logical_not(alone))
    def _():
        list_home.start()

    u = jnp.where(c == 1, b, 3 - b)

    def at_u(where):
        return dev(s, t, jnp.where(c == 1, where, 3 - where))

    def slot(at):
        return jnp.where(c == 1, at, 3 - at)

    cuts = up_send.shape[1]

    def cut(ref, r):
        return ref.at[:, pl.ds(0, head_size)] if r else ref.at[:, pl.ds(head_size, 2 * head_size)]

    def own(h, r, where):
        target = 3 if where == 2 else 2
        return remote(
            cut(w_in.at[h], r), cut(w_all.at[h, b], r), up_send.at[h, r], w_recv.at[b, h, r], at_u(target)
        )

    def forward(h, r, at):
        place = cut(w_all.at[h, slot(at)], r)
        return remote(place, place, fwd_send.at[at, h, r], w_recv.at[slot(at), h, r], at_u(3))

    def across(src, h, r, at):
        place = cut(w_all.at[h, slot(at)], r)
        return remote(src, place, core_send.at[at, h, r], w_recv.at[slot(at), h, r], partner)

    def arrived(h, r, place):
        return remote(
            cut(w_in.at[h], r), cut(w_all.at[h, place], r), up_send.at[h, r], w_recv.at[place, h, r], partner
        )

    keep = pltpu.make_async_copy(w_in, w_all.at[:, b], local.at[1])

    def begin(where):
        for h in range(heads):
            for i in range(3):
                load(h, i).wait()
            for r in range(cuts):
                own(h, r, where).start()
                if where >= 2:
                    across(cut(w_in.at[h], r), h, r, where).start()
        if where >= 2:
            keep.start()

    for where in range(4):

        @pl.when(u == where)
        def _(where=where):
            begin(where)

    def spread(src, q, k):
        targets = [dev(s, 2 * couple + q, b), dev(other, 2 * couple + q, b)]
        targets += [dev(s, 2 * lax.rem(couple + j, couples) + q, b) for j in range(1, couples)]
        copies = [
            remote(src, tok.at[e, t, k], p_send.at[q, k, n], p_recv.at[e, t, k], peer)
            for n, peer in enumerate(targets)
        ]
        return copies, pltpu.make_async_copy(src, tok.at[e, t, k], local_t.at[k])

    def send(src, q, k):
        copies, here = spread(src, q, k)
        for copy in copies[1:]:
            copy.start()

        @pl.when(c == q)
        def _():
            here.start()

        @pl.when(c != q)
        def _():
            copies[0].start()

    def landed(from_e, from_t2, k):
        return remote(
            part(0), tok.at[from_e, from_t2, k], p_send.at[0, 0, 0], p_recv.at[from_e, from_t2, k], partner
        )

    def turn(n, k):
        if k % 2:
            from_t2 = 2 * lax.rem(couple + 1 + n // 2, couples) + n % 2
            return landed(e, from_t2, k), remote(
                tok.at[e, from_t2, k], tok.at[e, from_t2, k], turn_send.at[k, n],
                p_recv.at[e, from_t2, k], dev(other, t, b),
            )
        from_t2, jump = 2 * couple + n % 2, 1 + n // 2
        return landed(1 - e, from_t2, k), remote(
            tok.at[1 - e, from_t2, k], tok.at[1 - e, from_t2, k], turn_send.at[k, n],
            p_recv.at[1 - e, from_t2, k], dev(s, 2 * lax.rem(couple + jump, couples) + c, b),
        )

    turns = 2 * (couples - 1)
    for k in range(pieces):
        for n in range(2):
            q = jnp.where(b < 2, n, 1 - n)
            source = 2 * (b % 2) + q

            @pl.when(source == b)
            def _(q=q, k=k):
                send(part(k), q, k)

            @pl.when(source != b)
            def _(q=q, k=k):
                remote(part(k), relay.at[q, k], z_send.at[0, k], z_recv.at[q, k], partner).wait_recv()
                send(relay.at[q, k], q, k)

    def serve_2(h, r):
        for at in (1, 0):
            arrived(h, r, slot(at)).wait_recv()
            forward(h, r, at).start()
            across(cut(w_all.at[h, slot(at)], r), h, r, at).start()
        arrived(h, r, slot(3)).wait_recv()
        across(cut(w_all.at[h, slot(3)], r), h, r, 3).start()

    def serve(h, r):
        @pl.when(u == 3)
        def _():
            for at in (2, 1, 0):
                arrived(h, r, slot(at)).wait_recv()
                across(cut(w_all.at[h, slot(at)], r), h, r, at).start()

        @pl.when(u < 2)
        def _():
            for at in range(4):
                arrived(h, r, at).wait_recv()

    def pass_on(k):
        for m in range(turns):
            here, on = turn(m, k)
            if k % 2 or m < 2:
                here.wait_recv()
            on.start()

    for h in range(heads - 1):
        for k in range(h * pieces // (heads - 1), (h + 1) * pieces // (heads - 1)):
            pass_on(k)

        @pl.when(u == 2)
        def _(h=h):
            for r in range(cuts):
                serve_2(h, r)

    out_width = total.shape[1]

    def out_block(h, from_t2, half):
        place = pl.multiple_of((2 * from_t2 + half) * head_size, head_size)
        return w_cols.at[h, pl.ds(place, head_size)]

    def out_own(h, half):
        rows = pl.ds((half * heads + h) * head_size, head_size)
        src = w_out.at[rows, pl.ds(pl.multiple_of(t * out_width, out_width), out_width)]
        return pltpu.make_async_copy(src, out_block(h, t, half), o_local.at[h, half])

    partner_step = 1 - 2 * c

    def out_partner(h, half):
        target = t + partner_step
        rows = pl.ds((half * heads + h) * head_size, head_size)
        src = w_out.at[rows, pl.ds(pl.multiple_of(target * out_width, out_width), out_width)]
        return remote(src, out_block(h, t, half), o_send.at[0, h, half], o_recv.at[h, t, half], partner)

    def out_far(j, core, h):
        target = 2 * lax.rem(couple + j, couples) + core
        rows = pl.ds(pl.multiple_of((e * heads + h) * head_size, head_size), head_size)
        src = w_out.at[rows, pl.ds(pl.multiple_of(target * out_width, out_width), out_width)]
        return remote(
            src, out_block(h, t, e), o_send.at[2 * j + core, h, 0], o_recv.at[h, t, e], dev(s, target, b)
        )

    def out_turn(j, core, h):
        from_t2 = 2 * lax.rem(couple + j, couples) + core
        block = out_block(h, from_t2, e)
        return remote(
            block, block, o_send.at[2 * j + core, h, 1], o_recv.at[h, from_t2, e], dev(other, t, b)
        )

    def turn_columns(h):
        for j in range(1, couples):
            for core in range(2):
                on = out_turn(j, core, h)
                on.wait_recv()
                on.start()

    for h in range(heads):
        for j in range(1, couples):
            for core in range(2):
                out_far(j, core, h).start()
        for half in range(2):
            out_partner(h, half).start()
            out_own(h, half).start()

    remote(lists_in, lists_v.at[1 - e], l_send.at[0], l_recv.at[1 - e], partner).wait_recv()

    @pl.when(alone)
    def _():
        list_here.wait()

    @pl.when(jnp.logical_not(alone))
    def _():
        remote(lists_in, lists_v.at[e], l_send.at[0], l_recv.at[e], partner).wait_recv()

    down = pltpu.make_async_copy(lists_v, lists_s, local.at[3])
    down.start()
    down.wait()

    def set_places(tile, carry):
        half, i = tile // tiles, tile % tiles
        for j in range(slots):
            listed = lists_s[half, i, j]
            near = listed // (4 * tiles) - base
            group = jnp.where(near < 0, 2, jnp.where(near > 1, 3, near))
            row = listed // tiles % 4 - band_here + 1
            place = (row * groups + group) * tiles + listed % tiles
            place_s[tile, j] = jnp.clip(place, 0, 3 * groups * tiles - 1)
        place_s[tile, slots] = lists_s[half, i, slots]
        return carry

    lax.fori_loop(0, 2 * tiles, set_places, 0)

    block = 64 if piece_rows % 64 == 0 else piece_rows
    many = piece_rows // block

    def norm_piece(n, carry):
        half, k = lax.rem(e + n // pieces, 2), n % pieces

        @pl.when(half == e)
        def _():
            @pl.when(k % 2 == 0)
            def _():
                for j in range(2, tps):
                    landed(e, lax.rem(2 * couple + j, tps), k).wait_recv()

            landed(e, t + 1 - 2 * c, k).wait_recv()
            spread(part(0), c, k)[1].wait()

        @pl.when(half != e)
        def _():
            @pl.when(k % 2 == 1)
            def _():
                for j in range(2):
                    landed(1 - e, 2 * couple + j, k).wait_recv()

            for j in range(2, tps):
                landed(1 - e, lax.rem(2 * couple + j, tps), k).wait_recv()

        def norm_rows(i, inner):
            rows = pl.ds(pl.multiple_of(i * block, block), block)
            floats = jnp.concatenate([tok[half, j, k, rows, :] for j in range(tps)], axis=1).astype(F32)
            moved = floats - jnp.mean(floats, axis=-1, keepdims=True)
            spread_of = jnp.mean(moved * moved, axis=-1, keepdims=True)
            at = ((half * pieces + k) * many + i) * block
            normed[pl.ds(pl.multiple_of(at, block), block), :] = (
                moved * lax.rsqrt(spread_of + 1e-06) * (1.0 + scale[...]) + shift[...]
            ).astype(BF)
            return inner

        lax.fori_loop(0, many, norm_rows, 0)
        return carry

    lax.fori_loop(0, 2 * pieces, norm_piece, 0)

    @pl.when(u >= 2)
    def _():
        keep.wait()

    home = groups * tiles

    def multiplied(h, half, first, last):
        rows = pl.ds(pl.multiple_of(half * tok_rows, tok_rows), tok_rows)
        weights = w_all[h, :, :, first:last].reshape(normed.shape[1], last - first)
        return rows, jnp.dot(normed[rows, :], weights, preferred_element_type=F32)

    def project_keys(h):
        def rows_of(half, carry):
            _, product = multiplied(h, half, head_size, 3 * head_size)
            keys = head_norm(product[:, :head_size], k_gain[...])
            values = product[:, head_size:].astype(BF)
            for i in range(tiles):
                part = slice(i * tile_len, (i + 1) * tile_len)
                kvs[h][home + half * tiles + i, :, :head_size] = keys[part]
                kvs[h][home + half * tiles + i, :, head_size:] = values[part]
            return carry

        lax.fori_loop(0, 2, rows_of, 0)

    def project_queries(h):
        def rows_of(half, carry):
            rows, product = multiplied(h, half, 0, head_size)
            queries[h, rows, :] = head_norm(product, q_gain[...])
            return carry

        lax.fori_loop(0, 2, rows_of, 0)

    def share(h, n):
        p, g = steps[n]
        peer, there = neighbour(p, g)
        if p == 0:
            first, count, group = home, 2 * tiles, 0
        else:
            first, count, group = home + (tiles if p == 1 else 0), tiles, (2 if p == 1 else 3)
        target = (1 - g) * home + group * tiles
        copy = remote(
            kvs[h].at[pl.ds(first, count)], kvs[h].at[pl.ds(target, count)],
            kv_send.at[h, n], kv_recv.at[h, n], peer,
        )
        return copy, there

    def share_all(h):
        for n in range(len(steps)):
            copy, there = share(h, n)

            @pl.when(there)
            def _(copy=copy):
                copy.start()

    def shared(h):
        for n, (p, g) in enumerate(steps):
            copy, _ = share(h, n)
            _, there = neighbour(-p, -g)

            @pl.when(there)
            def _(copy=copy):
                copy.wait_recv()

    def tile_rows(i):
        return pl.ds(i * tile_len if isinstance(i, int) else pl.multiple_of(i * tile_len, tile_len), tile_len)

    def deal(h, i):
        rows = tile_rows(i)
        place = joint.at[h, 2 * to_t + e, rows]
        home_copy = remote(att.at[h, e, rows], place, j_send.at[h, 0, i], j_recv.at[h, e, i], dev(s, to_t, to_b))
        here = pltpu.make_async_copy(att.at[h, e, rows], joint.at[h, 2 * t + e, rows], j_send.at[h, 0, i])
        away = remote(
            att.at[h, 1 - e, rows], place, j_send.at[h, 1, i], j_recv.at[h, e, i], dev(other, to_t, to_b)
        )
        return home_copy, here, away

    def start_deal(h, i):
        home_copy, here, away = deal(h, i)
        away.start()

        @pl.when(alone)
        def _():
            here.start()

        @pl.when(jnp.logical_not(alone))
        def _():
            home_copy.start()

    inverse = 1.0 / head_size**0.5
    pair = 2 * tile_len
    lane = lax.broadcasted_iota(jnp.int32, (1, pair), 1)

    def attend(h):
        kv = kvs[h]

        def near(tile, j, first):
            parts = []
            for i in range(2):
                at = place_s[tile, min(2 * j + i, slots - 1)]
                parts.append(kv[at, :, first : first + head_size])
            return jnp.concatenate(parts, axis=0)

        def tile_of(i, half):
            tile = half * tiles + i
            rows = pl.ds(pl.multiple_of(tile * tile_len, tile_len), tile_len)
            query = queries[h, rows, :]
            limit = place_s[tile, slots] * tile_len
            trips = (slots + 1) // 2
            top = None
            for j in range(trips):
                found = lax.dot_general(
                    query, near(tile, j, 0), (((1,), (1,)), ((), ())), preferred_element_type=F32
                )
                found = jnp.where(lane < limit - pair * j, found * inverse, -1e30)
                scores[half, :, j * pair : (j + 1) * pair] = found
                top = found if top is None else jnp.maximum(top, found)
            top = jnp.max(top, axis=-1, keepdims=True)
            total = result = None
            for j in range(trips):
                weights = jnp.exp(scores[half, :, j * pair : (j + 1) * pair] - top)
                total = weights if total is None else total + weights
                found = jnp.dot(weights.astype(BF), near(tile, j, head_size), preferred_element_type=F32)
                result = found if result is None else result + found
            result = result * (1.0 / jnp.sum(total, axis=-1, keepdims=True))
            att[h, half, pl.ds(pl.multiple_of(i * tile_len, tile_len), tile_len), :] = result.astype(BF)

        def both(i, carry):
            tile_of(i, 0)
            tile_of(i, 1)
            start_deal(h, i)
            return carry

        lax.fori_loop(0, tiles, both, 0)

    def hand(h, part_of, i, j):
        place = joint.at[h, 2 * t + part_of, tile_rows(i)]
        peer = partner if j == 0 else dev(s, lax.rem(t + 2 * j, tps), b)
        return remote(place, place, a_send.at[h, part_of, i, j], a_recv.at[h, 2 * t + part_of, i], peer)

    def handed(h, from_t2, part_of, i):
        place = joint.at[h, 2 * from_t2 + part_of, tile_rows(i)]
        return remote(
            place, place, r_send.at[h, part_of, i, from_t2 // 2], a_recv.at[h, 2 * from_t2 + part_of, i], partner
        )

    def hand_out(h):
        for i in range(tiles):
            for m in range(2):
                part_of = e if m == 0 else 1 - e

                def arrive():
                    place = joint.at[h, 2 * t + part_of, tile_rows(i)]
                    remote(place, place, j_send.at[h, 0, i], j_recv.at[h, part_of, i], partner).wait_recv()

                if m == 0:

                    @pl.when(alone)
                    def _():
                        deal(h, i)[1].wait()

                    @pl.when(jnp.logical_not(alone))
                    def _():
                        arrive()
                else:
                    arrive()
                for j in range(1, couples):
                    hand(h, part_of, i, j).start()
                hand(h, part_of, i, 0).start()

    def multiply(h):
        for i in range(tiles):
            for m in range(2):
                for j in range(1, couples):
                    came = handed(h, lax.rem(t + 2 * j, tps), m, i)
                    came.wait_recv()
                    came.start()
        for i in range(tiles):
            for m in range(2):
                for j in range(couples):
                    handed(h, lax.rem(t + 1 - 2 * c + 2 * j, tps), m, i).wait_recv()
        for half in range(2):
            out_own(h, half).wait()
            block = out_block(h, t + partner_step, half)
            remote(block, block, o_send.at[0, h, half], o_recv.at[h, t + partner_step, half], partner).wait_recv()
        for j in range(1, couples):
            for core in range(2):
                from_t2 = 2 * lax.rem(couple + j, couples) + core
                block = out_block(h, from_t2, 1 - e)
                remote(block, block, o_send.at[0, h, 0], o_recv.at[h, from_t2, 1 - e], partner).wait_recv()
        whole = jnp.concatenate([joint[h, i] for i in range(2 * tps)], axis=1)
        product = jnp.dot(whole, w_cols[h], preferred_element_type=F32)
        if h == 0:
            total[...] = product
        elif h < heads - 1:
            total[...] += product
        else:
            out[...] = total[...] + product

    last = heads - 1

    def project(h):
        serve(h, 0)
        project_keys(h)
        share_all(h)
        serve(h, 1)
        project_queries(h)

    for h in range(last):
        project(h)

    @pl.when(u == 2)
    def _():
        for r in range(cuts):
            serve_2(last, r)

    for h in range(last):
        turn_columns(h)
        shared(h)
        attend(h)
        if h:
            hand_out(h - 1)
    turn_columns(last)
    project(last)
    hand_out(last - 1)
    for h in range(last - 1):
        multiply(h)
    shared(last)
    attend(last)
    hand_out(last)
    multiply(last - 1)
    multiply(last)

    for where in range(4):

        @pl.when(u == where)
        def _(where=where):
            for h in range(heads):
                for r in range(cuts):
                    own(h, r, where).wait_send()
                    if where == 2:
                        for at in (1, 0):
                            forward(h, r, at).wait_send()
                    if where >= 2:
                        for at in range(4):
                            across(cut(w_in.at[h], r), h, r, at).wait_send()

    for i in range(2):

        @pl.when(planes[i] != b)
        def _(i=i):
            for k in range(pieces):
                leg(i, k).wait_send()

    for k in range(pieces):
        for q in range(2):
            copies, _ = spread(part(0), q, k)
            for copy in copies[1:]:
                copy.wait_send()

            @pl.when(c != q)
            def _(copy=copies[0]):
                copy.wait_send()

        for m in range(turns):
            turn(m, k)[1].wait_send()

    for h in range(heads):
        for i in range(tiles):
            home_copy, _, away = deal(h, i)
            away.wait_send()

            @pl.when(jnp.logical_not(alone))
            def _(home_copy=home_copy):
                home_copy.wait_send()

            for m in range(2):
                for j in range(couples):
                    hand(h, m, i, j).wait_send()
                for j in range(1, couples):
                    handed(h, lax.rem(t + 2 * j, tps), m, i).wait_send()

        for j in range(1, couples):
            for core in range(2):
                out_far(j, core, h).wait_send()
                out_turn(j, core, h).wait_send()
        for m in range(2):
            out_partner(h, m).wait_send()

    list_away.wait_send()

    @pl.when(jnp.logical_not(alone))
    def _():
        list_home.wait_send()

    for h in range(heads):
        for n in range(len(steps)):
            copy, there = share(h, n)

            @pl.when(there)
            def _(copy=copy):
                copy.wait_send()


def branch(tokens, w, scale, shift, q_gain, k_gain, ids, counts, w_out, slabs, tps):
    tok_rows, tok_width = tokens.shape
    tiles, slots = ids.shape
    head_size = q_gain.shape[0]
    heads, deep, wide = w.shape[2] // head_size // 2, w.shape[1], 3 * head_size
    tile_len = tok_rows // tiles
    width = scale.shape[0]
    pieces = 4 if tok_rows % 64 == 0 else 2
    cuts = 2
    groups = 4 if slabs > 2 else 2
    steps = 8 if slabs > 2 else 2
    dma = pltpu.SemaphoreType.DMA
    vmem = pl.BlockSpec(memory_space=pltpu.VMEM)
    smem = pl.BlockSpec(memory_space=pltpu.SMEM)
    lists = (8, 128)
    out_width = w_out.shape[1] // tps
    return pl.pallas_call(
        functools.partial(branch_kernel, (slabs, tps, heads, tiles, slots)),
        out_shape=jax.ShapeDtypeStruct((tok_rows, out_width), F32),
        in_specs=[pl.BlockSpec(memory_space=pl.ANY)] * 2 + [vmem] * 4 + [smem] * 2 + [pl.BlockSpec(memory_space=pl.ANY)],
        out_specs=vmem,
        scratch_shapes=[
            pltpu.VMEM(lists, jnp.int32),
            pltpu.VMEM((heads, deep, wide), BF),
            pltpu.VMEM((2, tps, pieces, tok_rows // pieces, tok_width), BF),
            pltpu.VMEM((heads, 4, deep, wide), BF),
            pltpu.VMEM((2, pieces, tok_rows // pieces, tok_width), BF),
            pltpu.VMEM((2 * tok_rows, width), BF),
            pltpu.VMEM((heads, 2 * tok_rows, head_size), BF),
            [pltpu.VMEM((3 * groups * tiles, tile_len, 2 * head_size), BF) for _ in range(heads)],
            pltpu.VMEM((heads, 2, tok_rows, head_size), BF),
            pltpu.VMEM((heads, 2 * tps, tok_rows, head_size), BF),
            pltpu.VMEM((heads, 2 * tps * head_size, out_width), BF),
            pltpu.VMEM((tok_rows, out_width), F32),
            pltpu.VMEM((2, tile_len, (slots + 1) // 2 * 2 * tile_len), F32),
            pltpu.VMEM((2,) + lists, jnp.int32),
            pltpu.SMEM((2,) + lists, jnp.int32),
            pltpu.SMEM((2 * tiles, slots + 1), jnp.int32),
            dma((2, pieces)), dma((2, pieces)), dma((2, pieces, tps)), dma((2, tps, pieces)),
            dma((pieces, tps)),
            dma((heads, cuts)), dma((2, heads, cuts)), dma((4, heads, cuts)), dma((4, heads, cuts)),
            dma((heads, steps)), dma((heads, steps)), dma((2,)), dma((2,)), dma((4,)), dma((pieces,)),
            dma((heads, 3)),
            dma((heads, 2, tiles)), dma((heads, 2, tiles)), dma((heads, 2, tiles, tps // 2)),
            dma((heads, 2 * tps, tiles)), dma((heads, 2, tiles, tps // 2)), dma((tps, heads, 2)), dma((heads, tps, 2)), dma((heads, 2)),
        ],
        compiler_params=pltpu.CompilerParams(
            collective_id=0, has_side_effects=True, vmem_limit_bytes=56 * 2**20
        ),
        name="branch",
    )(
        tokens, w, scale.reshape(1, -1), shift.reshape(1, -1), q_gain.reshape(1, -1),
        k_gain.reshape(1, -1), ids, counts, w_out,
    )


def shards(tokens, w_qkv, w_out, shift, scale, gate, q_gain, k_gain, tile_ids, key_counts):
    slabs, tps = lax.axis_size("slab"), lax.axis_size("tp")
    product = branch(
        tokens, w_qkv.transpose(1, 0, 2), scale, shift, q_gain, k_gain, tile_ids, key_counts, w_out,
        slabs, tps,
    )
    return (gate * product).astype(BF)


def solution(mesh):
    in_specs = (
        P(("slab", "band"), "tp"),
        P("band", None, "tp"),
        P("tp", None),
        P(),
        P(),
        P("tp"),
        P(),
        P(),
        P(("slab", "band"), None),
        P(("slab", "band")),
    )
    out_specs = P(("slab", "band"), "tp")
    return jax.shard_map(shards, mesh=mesh, in_specs=in_specs, out_specs=out_specs, check_vma=False)
```

```python
import functools

import jax
import jax.numpy as jnp
from jax import lax
from jax.experimental import pallas as pl
from jax.experimental.pallas import tpu as pltpu
from jax.sharding import PartitionSpec as P

BF = jnp.bfloat16
F32 = jnp.float32


def head_norm(piece, gain):
    squares = jnp.mean(piece * piece, axis=-1, keepdims=True)
    return (piece * lax.rsqrt(squares + 1e-06) * gain).astype(BF)


def branch_kernel(dims, tok_in, w_qkv, scale, shift, q_gain, k_gain, ids, counts, w_out, out, lists_in, w_in, tok, w_all,
                  relay, normed, queries, kvs, att, joint, w_cols, total, scores, lists_v, lists_s, place_s, z_send, z_recv, p_send,
                  p_recv, turn_send, up_send, fwd_send, core_send, w_recv, kv_send, kv_recv, l_send, l_recv,
                  local, local_t, w_sem,
                  j_send, j_recv, a_send, a_recv, r_send, o_send, o_recv, o_local):
    slabs, tps, heads, tiles, slots = dims
    s, t, b = lax.axis_index("slab"), lax.axis_index("tp"), lax.axis_index("band")
    e, c = s % 2, t % 2
    base = s - e
    couples, couple = tps // 2, t // 2
    kind = pl.DeviceIdType.MESH
    head_size = q_gain.shape[1]
    tok_rows, tok_width = tok_in.shape
    tile_len = tok_rows // tiles
    groups = 4 if slabs > 2 else 2
    band_here = 2 * (b % 2) + c
    alone = (c == b // 2) & (c == b % 2)
    other = s + 1 - 2 * e

    def dev(slab, tp, band):
        return {"slab": slab, "tp": tp, "band": band}

    def remote(src, dst, send, recv, peer):
        return pltpu.make_async_remote_copy(src, dst, send, recv, device_id=peer, device_id_type=kind)

    to_t, to_b = 2 * couple + b // 2, 2 * (b % 2) + c
    from_t, from_b = 2 * couple + b % 2, 2 * c + b // 2
    partner = dev(s, t + 1 - 2 * c, b)

    steps = [(0, 1), (0, -1)]
    if slabs > 2:
        steps += [(p, g) for p in (1, -1) for g in (0, 1, -1)]

    def neighbour(p, g):
        at = band_here + g
        there = (at >= 0) & (at <= 3)
        if p:
            there = there & (s + 2 * p >= 0) & (s + 2 * p < slabs)
        at = jnp.clip(at, 0, 3)
        slab = jnp.clip(s + 2 * p, 0, slabs - 1) if p else s
        return dev(slab, 2 * couple + at % 2, 2 * (b // 2) + at // 2), there

    def load(h, i):
        first = pl.multiple_of(e * heads * head_size + h * head_size, head_size)
        cols = slice(i * head_size, (i + 1) * head_size)
        return pltpu.make_async_copy(
            w_qkv.at[i, :, pl.ds(first, head_size)], w_in.at[h, :, cols], w_sem.at[h, i]
        )

    for h in range(heads):
        for i in range(3):
            load(h, i).start()

    barrier = pltpu.get_barrier_semaphore()

    def greet(peer):
        pl.semaphore_signal(barrier, inc=1, device_id=peer, device_id_type=kind)

    peers = [dev(s, t, (b + i) % 4) for i in range(1, 4)]
    for i in range(2):
        for j in range(tps):
            if i or j:
                peers.append(dev(base + (e + i) % 2, (t + j) % tps, b))
    peers += [dev(other, to_t, to_b), dev(other, from_t, from_b)]
    for peer in peers:
        greet(peer)
    expected = len(peers) + jnp.where(alone, 0, 2)

    @pl.when(jnp.logical_not(alone))
    def _():
        greet(dev(s, to_t, to_b))
        greet(dev(s, from_t, from_b))

    for p, g in steps:
        peer, there = neighbour(p, g)
        expected = expected + jnp.where(there, 1, 0)

        @pl.when(there)
        def _(peer=peer):
            greet(peer)

    pl.semaphore_wait(barrier, expected)

    pieces, piece_rows = tok.shape[2], tok.shape[3]
    planes = [b // 2, 2 + b // 2]

    def part(k):
        return tok_in.at[pl.ds(k * piece_rows, piece_rows)]

    def leg(i, k):
        return remote(
            part(k), relay.at[b % 2, k], z_send.at[i, k], z_recv.at[b % 2, k], dev(s, t, planes[i])
        )

    far_first = [1, 0]
    for i in far_first:

        @pl.when(planes[i] != b)
        def _(i=i):
            for k in range(pieces):
                leg(i, k).start()

    row_of = lax.broadcasted_iota(jnp.int32, lists_in.shape, 0)
    col_of = lax.broadcasted_iota(jnp.int32, lists_in.shape, 1)
    packed = jnp.zeros(lists_in.shape, jnp.int32)
    for i in range(tiles):
        for j in range(slots + 1):
            entry = ids[i, j] if j < slots else counts[i]
            packed = jnp.where((row_of == i) & (col_of == j), entry, packed)
    lists_in[...] = packed
    list_home = remote(lists_in, lists_v.at[e], l_send.at[0], l_recv.at[e], dev(s, from_t, from_b))
    list_away = remote(lists_in, lists_v.at[e], l_send.at[1], l_recv.at[e], dev(other, from_t, from_b))
    list_here = pltpu.make_async_copy(lists_in, lists_v.at[e], local.at[0])
    list_away.start()

    @pl.when(alone)
    def _():
        list_here.start()

    @pl.when(jnp.logical_not(alone))
    def _():
        list_home.start()

    u = jnp.where(c == 1, b, 3 - b)

    def at_u(where):
        return dev(s, t, jnp.where(c == 1, where, 3 - where))

    def slot(at):
        return jnp.where(c == 1, at, 3 - at)

    cuts = up_send.shape[1]

    def cut(ref, r):
        return ref.at[:, pl.ds(0, head_size)] if r else ref.at[:, pl.ds(head_size, 2 * head_size)]

    def own(h, r, where):
        target = 3 if where == 2 else 2
        return remote(
            cut(w_in.at[h], r), cut(w_all.at[h, b], r), up_send.at[h, r], w_recv.at[b, h, r], at_u(target)
        )

    def forward(h, r, at):
        place = cut(w_all.at[h, slot(at)], r)
        return remote(place, place, fwd_send.at[at, h, r], w_recv.at[slot(at), h, r], at_u(3))

    def across(src, h, r, at):
        place = cut(w_all.at[h, slot(at)], r)
        return remote(src, place, core_send.at[at, h, r], w_recv.at[slot(at), h, r], partner)

    def arrived(h, r, place):
        return remote(
            cut(w_in.at[h], r), cut(w_all.at[h, place], r), up_send.at[h, r], w_recv.at[place, h, r], partner
        )

    keep = pltpu.make_async_copy(w_in, w_all.at[:, b], local.at[1])

    def begin(where):
        for h in range(heads):
            for i in range(3):
                load(h, i).wait()
            for r in range(cuts):
                own(h, r, where).start()
                if where >= 2:
                    across(cut(w_in.at[h], r), h, r, where).start()
        if where >= 2:
            keep.start()

    for where in range(4):

        @pl.when(u == where)
        def _(where=where):
            begin(where)

    def spread(src, q, k):
        targets = [dev(s, 2 * couple + q, b), dev(other, 2 * couple + q, b)]
        targets += [dev(s, 2 * lax.rem(couple + j, couples) + q, b) for j in range(1, couples)]
        copies = [
            remote(src, tok.at[e, t, k], p_send.at[q, k, n], p_recv.at[e, t, k], peer)
            for n, peer in enumerate(targets)
        ]
        return copies, pltpu.make_async_copy(src, tok.at[e, t, k], local_t.at[k])

    def send(src, q, k):
        copies, here = spread(src, q, k)
        for copy in copies[1:]:
            copy.start()

        @pl.when(c == q)
        def _():
            here.start()

        @pl.when(c != q)
        def _():
            copies[0].start()

    def landed(from_e, from_t2, k):
        return remote(
            part(0), tok.at[from_e, from_t2, k], p_send.at[0, 0, 0], p_recv.at[from_e, from_t2, k], partner
        )

    def turn(n, k):
        if k % 2:
            from_t2 = 2 * lax.rem(couple + 1 + n // 2, couples) + n % 2
            return landed(e, from_t2, k), remote(
                tok.at[e, from_t2, k], tok.at[e, from_t2, k], turn_send.at[k, n],
                p_recv.at[e, from_t2, k], dev(other, t, b),
            )
        from_t2, jump = 2 * couple + n % 2, 1 + n // 2
        return landed(1 - e, from_t2, k), remote(
            tok.at[1 - e, from_t2, k], tok.at[1 - e, from_t2, k], turn_send.at[k, n],
            p_recv.at[1 - e, from_t2, k], dev(s, 2 * lax.rem(couple + jump, couples) + c, b),
        )

    turns = 2 * (couples - 1)
    for k in range(pieces):
        for n in range(2):
            q = jnp.where(b < 2, n, 1 - n)
            source = 2 * (b % 2) + q

            @pl.when(source == b)
            def _(q=q, k=k):
                send(part(k), q, k)

            @pl.when(source != b)
            def _(q=q, k=k):
                remote(part(k), relay.at[q, k], z_send.at[0, k], z_recv.at[q, k], partner).wait_recv()
                send(relay.at[q, k], q, k)

    def serve_2(h, r):
        for at in (1, 0):
            arrived(h, r, slot(at)).wait_recv()
            forward(h, r, at).start()
            across(cut(w_all.at[h, slot(at)], r), h, r, at).start()
        arrived(h, r, slot(3)).wait_recv()
        across(cut(w_all.at[h, slot(3)], r), h, r, 3).start()

    def serve(h, r):
        @pl.when(u == 3)
        def _():
            for at in (2, 1, 0):
                arrived(h, r, slot(at)).wait_recv()
                across(cut(w_all.at[h, slot(at)], r), h, r, at).start()

        @pl.when(u < 2)
        def _():
            for at in range(4):
                arrived(h, r, at).wait_recv()

    def pass_on(k):
        for m in range(turns):
            here, on = turn(m, k)
            if k % 2 or m < 2:
                here.wait_recv()
            on.start()

    for h in range(heads - 1):
        for k in range(h * pieces // (heads - 1), (h + 1) * pieces // (heads - 1)):
            pass_on(k)

        @pl.when(u == 2)
        def _(h=h):
            for r in range(cuts):
                serve_2(h, r)

    out_width = total.shape[1]

    def out_block(h, from_t2, half):
        place = pl.multiple_of((2 * from_t2 + half) * head_size, head_size)
        return w_cols.at[h, pl.ds(place, head_size)]

    def out_own(h, half):
        rows = pl.ds((half * heads + h) * head_size, head_size)
        src = w_out.at[rows, pl.ds(pl.multiple_of(t * out_width, out_width), out_width)]
        return pltpu.make_async_copy(src, out_block(h, t, half), o_local.at[h, half])

    partner_step = 1 - 2 * c

    def out_partner(h, half):
        target = t + partner_step
        rows = pl.ds((half * heads + h) * head_size, head_size)
        src = w_out.at[rows, pl.ds(pl.multiple_of(target * out_width, out_width), out_width)]
        return remote(src, out_block(h, t, half), o_send.at[0, h, half], o_recv.at[h, t, half], partner)

    def out_far(j, core, h):
        target = 2 * lax.rem(couple + j, couples) + core
        rows = pl.ds(pl.multiple_of((e * heads + h) * head_size, head_size), head_size)
        src = w_out.at[rows, pl.ds(pl.multiple_of(target * out_width, out_width), out_width)]
        return remote(
            src, out_block(h, t, e), o_send.at[2 * j + core, h, 0], o_recv.at[h, t, e], dev(s, target, b)
        )

    def out_turn(j, core, h):
        from_t2 = 2 * lax.rem(couple + j, couples) + core
        block = out_block(h, from_t2, e)
        return remote(
            block, block, o_send.at[2 * j + core, h, 1], o_recv.at[h, from_t2, e], dev(other, t, b)
        )

    def turn_columns(h):
        for j in range(1, couples):
            for core in range(2):
                on = out_turn(j, core, h)
                on.wait_recv()
                on.start()

    for h in range(heads):
        for j in range(1, couples):
            for core in range(2):
                out_far(j, core, h).start()
        for half in range(2):
            out_partner(h, half).start()
            out_own(h, half).start()

    remote(lists_in, lists_v.at[1 - e], l_send.at[0], l_recv.at[1 - e], partner).wait_recv()

    @pl.when(alone)
    def _():
        list_here.wait()

    @pl.when(jnp.logical_not(alone))
    def _():
        remote(lists_in, lists_v.at[e], l_send.at[0], l_recv.at[e], partner).wait_recv()

    down = pltpu.make_async_copy(lists_v, lists_s, local.at[3])
    down.start()
    down.wait()

    def set_places(tile, carry):
        half, i = tile // tiles, tile % tiles
        for j in range(slots):
            listed = lists_s[half, i, j]
            near = listed // (4 * tiles) - base
            group = jnp.where(near < 0, 2, jnp.where(near > 1, 3, near))
            row = listed // tiles % 4 - band_here + 1
            place = (row * groups + group) * tiles + listed % tiles
            place_s[tile, j] = jnp.clip(place, 0, 3 * groups * tiles - 1)
        place_s[tile, slots] = lists_s[half, i, slots]
        return carry

    lax.fori_loop(0, 2 * tiles, set_places, 0)

    block = 64 if piece_rows % 64 == 0 else piece_rows
    many = piece_rows // block

    def norm_piece(n, carry):
        half, k = lax.rem(e + n // pieces, 2), n % pieces

        @pl.when(half == e)
        def _():
            @pl.when(k % 2 == 0)
            def _():
                for j in range(2, tps):
                    landed(e, lax.rem(2 * couple + j, tps), k).wait_recv()

            landed(e, t + 1 - 2 * c, k).wait_recv()
            spread(part(0), c, k)[1].wait()

        @pl.when(half != e)
        def _():
            @pl.when(k % 2 == 1)
            def _():
                for j in range(2):
                    landed(1 - e, 2 * couple + j, k).wait_recv()

            for j in range(2, tps):
                landed(1 - e, lax.rem(2 * couple + j, tps), k).wait_recv()

        def norm_rows(i, inner):
            rows = pl.ds(pl.multiple_of(i * block, block), block)
            floats = jnp.concatenate([tok[half, j, k, rows, :] for j in range(tps)], axis=1).astype(F32)
            moved = floats - jnp.mean(floats, axis=-1, keepdims=True)
            spread_of = jnp.mean(moved * moved, axis=-1, keepdims=True)
            at = ((half * pieces + k) * many + i) * block
            normed[pl.ds(pl.multiple_of(at, block), block), :] = (
                moved * lax.rsqrt(spread_of + 1e-06) * (1.0 + scale[...]) + shift[...]
            ).astype(BF)
            return inner

        lax.fori_loop(0, many, norm_rows, 0)
        return carry

    lax.fori_loop(0, 2 * pieces, norm_piece, 0)

    @pl.when(u >= 2)
    def _():
        keep.wait()

    home = groups * tiles

    def multiplied(h, half, first, last):
        rows = pl.ds(pl.multiple_of(half * tok_rows, tok_rows), tok_rows)
        weights = w_all[h, :, :, first:last].reshape(normed.shape[1], last - first)
        return rows, jnp.dot(normed[rows, :], weights, preferred_element_type=F32)

    def project_keys(h):
        def rows_of(half, carry):
            _, product = multiplied(h, half, head_size, 3 * head_size)
            keys = head_norm(product[:, :head_size], k_gain[...])
            values = product[:, head_size:].astype(BF)
            for i in range(tiles):
                part = slice(i * tile_len, (i + 1) * tile_len)
                kvs[h][home + half * tiles + i, :, :head_size] = keys[part]
                kvs[h][home + half * tiles + i, :, head_size:] = values[part]
            return carry

        lax.fori_loop(0, 2, rows_of, 0)

    def project_queries(h):
        def rows_of(half, carry):
            rows, product = multiplied(h, half, 0, head_size)
            queries[h, rows, :] = head_norm(product, q_gain[...])
            return carry

        lax.fori_loop(0, 2, rows_of, 0)

    def share(h, n):
        p, g = steps[n]
        peer, there = neighbour(p, g)
        if p == 0:
            first, count, group = home, 2 * tiles, 0
        else:
            first, count, group = home + (tiles if p == 1 else 0), tiles, (2 if p == 1 else 3)
        target = (1 - g) * home + group * tiles
        copy = remote(
            kvs[h].at[pl.ds(first, count)], kvs[h].at[pl.ds(target, count)],
            kv_send.at[h, n], kv_recv.at[h, n], peer,
        )
        return copy, there

    def share_all(h):
        for n in range(len(steps)):
            copy, there = share(h, n)

            @pl.when(there)
            def _(copy=copy):
                copy.start()

    def shared(h):
        for n, (p, g) in enumerate(steps):
            copy, _ = share(h, n)
            _, there = neighbour(-p, -g)

            @pl.when(there)
            def _(copy=copy):
                copy.wait_recv()

    def tile_rows(i):
        return pl.ds(i * tile_len if isinstance(i, int) else pl.multiple_of(i * tile_len, tile_len), tile_len)

    def deal(h, i):
        rows = tile_rows(i)
        place = joint.at[h, 2 * to_t + e, rows]
        home_copy = remote(att.at[h, e, rows], place, j_send.at[h, 0, i], j_recv.at[h, e, i], dev(s, to_t, to_b))
        here = pltpu.make_async_copy(att.at[h, e, rows], joint.at[h, 2 * t + e, rows], j_send.at[h, 0, i])
        away = remote(
            att.at[h, 1 - e, rows], place, j_send.at[h, 1, i], j_recv.at[h, e, i], dev(other, to_t, to_b)
        )
        return home_copy, here, away

    def start_deal(h, i):
        home_copy, here, away = deal(h, i)
        away.start()

        @pl.when(alone)
        def _():
            here.start()

        @pl.when(jnp.logical_not(alone))
        def _():
            home_copy.start()

    inverse = 1.0 / head_size**0.5
    pair = 2 * tile_len
    lane = lax.broadcasted_iota(jnp.int32, (1, pair), 1)

    def attend(h):
        kv = kvs[h]

        def near(tile, j, first):
            parts = []
            for i in range(2):
                at = place_s[tile, min(2 * j + i, slots - 1)]
                parts.append(kv[at, :, first : first + head_size])
            return jnp.concatenate(parts, axis=0)

        def tile_of(i, half):
            tile = half * tiles + i
            rows = pl.ds(pl.multiple_of(tile * tile_len, tile_len), tile_len)
            query = queries[h, rows, :]
            limit = place_s[tile, slots] * tile_len
            trips = (slots + 1) // 2
            top = None
            for j in range(trips):
                found = lax.dot_general(
                    query, near(tile, j, 0), (((1,), (1,)), ((), ())), preferred_element_type=F32
                )
                found = jnp.where(lane < limit - pair * j, found * inverse, -1e30)
                scores[half, :, j * pair : (j + 1) * pair] = found
                top = found if top is None else jnp.maximum(top, found)
            top = jnp.max(top, axis=-1, keepdims=True)
            total = None
            for j in range(trips):
                weights = jnp.exp(scores[half, :, j * pair : (j + 1) * pair] - top)
                scores[half, :, j * pair : (j + 1) * pair] = weights
                total = weights if total is None else total + weights
            part = 1.0 / jnp.sum(total, axis=-1, keepdims=True)
            result = None
            for j in range(trips):
                probs = (scores[half, :, j * pair : (j + 1) * pair] * part).astype(BF)
                found = jnp.dot(probs, near(tile, j, head_size), preferred_element_type=F32)
                result = found if result is None else result + found
            att[h, half, pl.ds(pl.multiple_of(i * tile_len, tile_len), tile_len), :] = result.astype(BF)

        def both(i, carry):
            tile_of(i, 0)
            tile_of(i, 1)
            start_deal(h, i)
            return carry

        lax.fori_loop(0, tiles, both, 0)

    def hand(h, part_of, i, j):
        place = joint.at[h, 2 * t + part_of, tile_rows(i)]
        peer = partner if j == 0 else dev(s, lax.rem(t + 2 * j, tps), b)
        return remote(place, place, a_send.at[h, part_of, i, j], a_recv.at[h, 2 * t + part_of, i], peer)

    def handed(h, from_t2, part_of, i):
        place = joint.at[h, 2 * from_t2 + part_of, tile_rows(i)]
        return remote(
            place, place, r_send.at[h, part_of, i, from_t2 // 2], a_recv.at[h, 2 * from_t2 + part_of, i], partner
        )

    def hand_out(h):
        for i in range(tiles):
            for m in range(2):
                part_of = e if m == 0 else 1 - e

                def arrive():
                    place = joint.at[h, 2 * t + part_of, tile_rows(i)]
                    remote(place, place, j_send.at[h, 0, i], j_recv.at[h, part_of, i], partner).wait_recv()

                if m == 0:

                    @pl.when(alone)
                    def _():
                        deal(h, i)[1].wait()

                    @pl.when(jnp.logical_not(alone))
                    def _():
                        arrive()
                else:
                    arrive()
                for j in range(1, couples):
                    hand(h, part_of, i, j).start()
                hand(h, part_of, i, 0).start()

    def multiply(h):
        for i in range(tiles):
            for m in range(2):
                for j in range(1, couples):
                    came = handed(h, lax.rem(t + 2 * j, tps), m, i)
                    came.wait_recv()
                    came.start()
        for i in range(tiles):
            for m in range(2):
                for j in range(couples):
                    handed(h, lax.rem(t + 1 - 2 * c + 2 * j, tps), m, i).wait_recv()
        for half in range(2):
            out_own(h, half).wait()
            block = out_block(h, t + partner_step, half)
            remote(block, block, o_send.at[0, h, half], o_recv.at[h, t + partner_step, half], partner).wait_recv()
        for j in range(1, couples):
            for core in range(2):
                from_t2 = 2 * lax.rem(couple + j, couples) + core
                block = out_block(h, from_t2, 1 - e)
                remote(block, block, o_send.at[0, h, 0], o_recv.at[h, from_t2, 1 - e], partner).wait_recv()
        whole = jnp.concatenate([joint[h, i] for i in range(2 * tps)], axis=1)
        product = jnp.dot(whole, w_cols[h], preferred_element_type=F32)
        if h == 0:
            total[...] = product
        elif h < heads - 1:
            total[...] += product
        else:
            out[...] = total[...] + product

    last = heads - 1

    def project(h):
        serve(h, 0)
        project_keys(h)
        share_all(h)
        serve(h, 1)
        project_queries(h)

    for h in range(last):
        project(h)

    @pl.when(u == 2)
    def _():
        for r in range(cuts):
            serve_2(last, r)

    for h in range(last):
        turn_columns(h)
        shared(h)
        attend(h)
        if h:
            hand_out(h - 1)
    turn_columns(last)
    project(last)
    hand_out(last - 1)
    for h in range(last - 1):
        multiply(h)
    shared(last)
    attend(last)
    hand_out(last)
    multiply(last - 1)
    multiply(last)

    for where in range(4):

        @pl.when(u == where)
        def _(where=where):
            for h in range(heads):
                for r in range(cuts):
                    own(h, r, where).wait_send()
                    if where == 2:
                        for at in (1, 0):
                            forward(h, r, at).wait_send()
                    if where >= 2:
                        for at in range(4):
                            across(cut(w_in.at[h], r), h, r, at).wait_send()

    for i in range(2):

        @pl.when(planes[i] != b)
        def _(i=i):
            for k in range(pieces):
                leg(i, k).wait_send()

    for k in range(pieces):
        for q in range(2):
            copies, _ = spread(part(0), q, k)
            for copy in copies[1:]:
                copy.wait_send()

            @pl.when(c != q)
            def _(copy=copies[0]):
                copy.wait_send()

        for m in range(turns):
            turn(m, k)[1].wait_send()

    for h in range(heads):
        for i in range(tiles):
            home_copy, _, away = deal(h, i)
            away.wait_send()

            @pl.when(jnp.logical_not(alone))
            def _(home_copy=home_copy):
                home_copy.wait_send()

            for m in range(2):
                for j in range(couples):
                    hand(h, m, i, j).wait_send()
                for j in range(1, couples):
                    handed(h, lax.rem(t + 2 * j, tps), m, i).wait_send()

        for j in range(1, couples):
            for core in range(2):
                out_far(j, core, h).wait_send()
                out_turn(j, core, h).wait_send()
        for m in range(2):
            out_partner(h, m).wait_send()

    list_away.wait_send()

    @pl.when(jnp.logical_not(alone))
    def _():
        list_home.wait_send()

    for h in range(heads):
        for n in range(len(steps)):
            copy, there = share(h, n)

            @pl.when(there)
            def _(copy=copy):
                copy.wait_send()


def branch(tokens, w, scale, shift, q_gain, k_gain, ids, counts, w_out, slabs, tps):
    tok_rows, tok_width = tokens.shape
    tiles, slots = ids.shape
    head_size = q_gain.shape[0]
    heads, deep, wide = w.shape[2] // head_size // 2, w.shape[1], 3 * head_size
    tile_len = tok_rows // tiles
    width = scale.shape[0]
    pieces = 6 if tok_rows % 96 == 0 else 2
    cuts = 2
    groups = 4 if slabs > 2 else 2
    steps = 8 if slabs > 2 else 2
    dma = pltpu.SemaphoreType.DMA
    vmem = pl.BlockSpec(memory_space=pltpu.VMEM)
    smem = pl.BlockSpec(memory_space=pltpu.SMEM)
    lists = (8, 128)
    out_width = w_out.shape[1] // tps
    return pl.pallas_call(
        functools.partial(branch_kernel, (slabs, tps, heads, tiles, slots)),
        out_shape=jax.ShapeDtypeStruct((tok_rows, out_width), F32),
        in_specs=[vmem, pl.BlockSpec(memory_space=pl.ANY)] + [vmem] * 4 + [smem] * 2 + [pl.BlockSpec(memory_space=pl.ANY)],
        out_specs=vmem,
        scratch_shapes=[
            pltpu.VMEM(lists, jnp.int32),
            pltpu.VMEM((heads, deep, wide), BF),
            pltpu.VMEM((2, tps, pieces, tok_rows // pieces, tok_width), BF),
            pltpu.VMEM((heads, 4, deep, wide), BF),
            pltpu.VMEM((2, pieces, tok_rows // pieces, tok_width), BF),
            pltpu.VMEM((2 * tok_rows, width), BF),
            pltpu.VMEM((heads, 2 * tok_rows, head_size), BF),
            [pltpu.VMEM((3 * groups * tiles, tile_len, 2 * head_size), BF) for _ in range(heads)],
            pltpu.VMEM((heads, 2, tok_rows, head_size), BF),
            pltpu.VMEM((heads, 2 * tps, tok_rows, head_size), BF),
            pltpu.VMEM((heads, 2 * tps * head_size, out_width), BF),
            pltpu.VMEM((tok_rows, out_width), F32),
            pltpu.VMEM((2, tile_len, (slots + 1) // 2 * 2 * tile_len), F32),
            pltpu.VMEM((2,) + lists, jnp.int32),
            pltpu.SMEM((2,) + lists, jnp.int32),
            pltpu.SMEM((2 * tiles, slots + 1), jnp.int32),
            dma((2, pieces)), dma((2, pieces)), dma((2, pieces, tps)), dma((2, tps, pieces)),
            dma((pieces, tps)),
            dma((heads, cuts)), dma((2, heads, cuts)), dma((4, heads, cuts)), dma((4, heads, cuts)),
            dma((heads, steps)), dma((heads, steps)), dma((2,)), dma((2,)), dma((4,)), dma((pieces,)),
            dma((heads, 3)),
            dma((heads, 2, tiles)), dma((heads, 2, tiles)), dma((heads, 2, tiles, tps // 2)),
            dma((heads, 2 * tps, tiles)), dma((heads, 2, tiles, tps // 2)), dma((tps, heads, 2)), dma((heads, tps, 2)), dma((heads, 2)),
        ],
        compiler_params=pltpu.CompilerParams(
            collective_id=0, has_side_effects=True, vmem_limit_bytes=56 * 2**20
        ),
        name="branch",
    )(
        tokens, w, scale.reshape(1, -1), shift.reshape(1, -1), q_gain.reshape(1, -1),
        k_gain.reshape(1, -1), ids, counts, w_out,
    )


def shards(tokens, w_qkv, w_out, shift, scale, gate, q_gain, k_gain, tile_ids, key_counts):
    slabs, tps = lax.axis_size("slab"), lax.axis_size("tp")
    product = branch(
        tokens, w_qkv.transpose(1, 0, 2), scale, shift, q_gain, k_gain, tile_ids, key_counts, w_out,
        slabs, tps,
    )
    return (gate * product).astype(BF)


def solution(mesh):
    in_specs = (
        P(("slab", "band"), "tp"),
        P("band", None, "tp"),
        P("tp", None),
        P(),
        P(),
        P("tp"),
        P(),
        P(),
        P(("slab", "band"), None),
        P(("slab", "band")),
    )
    out_specs = P(("slab", "band"), "tp")
    return jax.shard_map(shards, mesh=mesh, in_specs=in_specs, out_specs=out_specs, check_vma=False)
```
